128 devices in a mesh: rep: 32 (over z, x, core), tp: 4 (over y).
Axes of the slice: x: 4, y: 4, z: 4, core: 2. Of those that a mesh axis runs over, the one named last changes fastest.
Arguments:
- hidden_in: bfloat16 [4096, 2048], P('rep'), may hold values from -6 to 6
- new_lengths: int32 [32, 4], P('rep'), may hold values from 1 to 64, 128 in all within a row
- prefix_lengths: int32 [32, 4], P('rep'), may hold values from 1 to 512, 1024 in all within a row
- cache_keys: bfloat16 [32768, 2048], P('rep', 'tp'), may hold values from -6 to 6
- cache_values: bfloat16 [32768, 2048], P('rep', 'tp'), may hold values from -6 to 6
- attn_gain: float32 [2048], replicated, may hold values from 0.1 to 1.9
- w_qkv: bfloat16 [2048, 3, 2048], P(None, None, 'tp'), may hold values from -1 to 1
- norm_gains: float32 [2, 2048], P(None, 'tp'), may hold values from 0 to 11
- w_out: bfloat16 [2048, 2048], P('tp'), may hold values from -0.125 to 0.125
- moe_gain: float32 [2048], replicated, may hold values from 0.1 to 1.9
- expert_ids: int32 [4096, 8], P('rep'), may hold values from 0 to 63, all different within a row; in each aligned block of 32 rows (0 to 31, 32 to 63, ...) at most 6 rows name the same one
- expert_weights: float32 [4096, 8], P('rep'), may hold values from 0.05 to 0.5
- w_gate_up: bfloat16 [64, 2048, 2, 1024], P('rep', None, None, 'tp'), may hold values from -0.125 to 0.125
- w_down: bfloat16 [64, 1024, 2048], P('rep', 'tp'), may hold values from -0.1875 to 0.1875
- next_gain: float32 [2048], replicated, may hold values from 0.1 to 1.9
- next_qkv: bfloat16 [2048, 3, 2048], P(None, None, 'tp'), may hold values from -1 to 1
- next_norm_gains: float32 [2, 2048], P(None, 'tp'), may hold values from 0.1 to 1.9
Outputs:
- hidden_out: bfloat16 [4096, 2048], P('rep')
- next_qkv_out: bfloat16 [4096, 3, 2048], P('rep', None, 'tp')
The draws below stay inside these ranges and needn't reach their ends.
Inputs may be any that keep to these rules, and one draw needn't show every extreme that they name: `expert_ids`: in every aligned block of 32 tokens no expert is chosen more than 6 times, and some block reaches 6; a token's 8 experts differ. `new_lengths`: each replica's lengths sum to 128; its longest request has exactly 64 new tokens. `prefix_lengths`: each replica's prefix lengths sum to 1024; its longest prefix has exactly 512 tokens.
All inputs are finite; a program needn't handle non-finite values.
Results may differ from the reference program's by a relative error of at most 0.023.
Values may be sent and summed in bfloat16 or wider, within the bound.
A program may use at most 128 MiB of HBM per device.

```python
import math
import jax
import jax.numpy as jnp
import numpy as np
from jax import lax

D = 2048
HD = 128
FF = 1024
TOP = 8
REQ = 4
ROWS = 128
CACHE_ROWS = 1024
EXPERTS = 64
TOKENS = 4096
NEW_MOST = 64
PREF_MOST = 512
QROWS = 32
CAPQ = 6
FF_TP = 256
N_REP = 32
N_TP = 4


def projection_draw(key, salt):
    draw_key = jax.random.fold_in(key, salt)
    columns = jnp.arange(D, dtype=jnp.float32) / (D - 1)
    entries = jnp.clip(jax.random.normal(draw_key, (D, 3, D), jnp.float32), -4.0, 4.0)
    growth = 3.0 ** (0.5 * columns)
    scales = jnp.stack([growth, growth, jnp.ones_like(growth)], axis=0)
    return entries * scales[None, :, :] * (1.0 / math.sqrt(D))


def draw_w_qkv(key, part):
    return projection_draw(key, 13).astype(jnp.bfloat16)


def draw_next_qkv(key, part):
    return projection_draw(key, 19).astype(jnp.bfloat16)


def draw_norm_gains(key, part):
    noise_key = jax.random.fold_in(jax.random.fold_in(key, 29), 0)
    return 1.0 + 0.18 * jnp.clip(jax.random.normal(noise_key, (2, D), jnp.float32), -4.0, 4.0)


def draw_hidden_in(key, part):
    lead_key = jax.random.fold_in(jax.random.fold_in(key, 5), 0)
    return jnp.clip(jax.random.normal(lead_key, (TOKENS, D), jnp.float32), -6.0, 6.0).astype(jnp.bfloat16)


def block_levels(rng, shape, cuts, low, largest):
    def one(dim, shards_of):
        draws = jax.random.uniform(jax.random.fold_in(jax.random.fold_in(rng, 6), dim), (shards_of,), jnp.float32, low / len(cuts), largest / len(cuts))
        return jnp.repeat(jnp.exp(draws), shape[dim] // shards_of).reshape((-1,) + (1,) * (len(shape) - dim - 1))

    loudness = one(*cuts[0])
    for cut in cuts[1:]:
        loudness = loudness * one(*cut)
    return loudness


def profile(number_of, total, reach, slope):
    loads = [(1 << 20) // math.isqrt(rank ** slope) + 1 for rank in range(2, number_of + 1)]
    spare, holding = total - reach - (number_of - 1), [1] * (number_of - 1)
    while spare > 0:
        movable = [i for i in range(number_of - 1) if holding[i] < reach]
        pool, budget = sum([loads[i] for i in movable]), spare
        for i in movable:
            extra = min(reach - holding[i], max(1, budget * loads[i] // pool), spare)
            holding[i] = holding[i] + extra
            spare = spare - extra
    return np.array([reach] + holding)


def uneven_parts(own_key, number_of, total, reach, skew):
    if number_of == 2:
        one = jax.random.randint(own_key, (), max(1, total - reach), min(reach, total - 1) + 1)
        return jnp.stack([one, total - one])
    sizes = jnp.asarray(profile(number_of, total, reach, skew), jnp.int32)
    couples = (number_of - 1) // 2
    donor, receiver = sizes[1:1 + 2 * couples:2], sizes[2:2 + 2 * couples:2]
    margin = jnp.minimum(donor - 1, reach - receiver)
    shifted = jax.random.randint(jax.random.fold_in(own_key, 1), (couples,), 0, 1 << 20) % (margin + 1)
    sizes = sizes.at[1:1 + 2 * couples:2].set(donor - shifted).at[2:2 + 2 * couples:2].set(receiver + shifted)
    return sizes[jax.random.permutation(jax.random.fold_in(own_key, 2), number_of)]


def deal_out(own_key, own, number, rows, amount, top, limit, slope):
    order = jax.random.permutation(own_key, amount)
    crowded, usual = load_shares(amount, rows * top, limit, slope, True), load_shares(amount, rows * top, limit, slope, False)
    places = jnp.arange(amount)

    def named(sizes, rotation):
        used = int((sizes > 0).sum())
        fixed = max(1, used // 4)
        shifted = fixed + (places - fixed + rotation * (used - fixed)) % max(1, amount - fixed)
        return jnp.zeros((amount,), jnp.int32).at[order[jnp.where(places < fixed, places, shifted)]].set(jnp.asarray(sizes, jnp.int32))

    sizes = jnp.where(number % 4 == 0, named(crowded, number // 4), named(usual, number - number // 4 - 1))
    mixed = jax.random.permutation(jax.random.fold_in(own, 3), amount)
    giver, taker = mixed[0:amount // 2 * 2:2], mixed[1:amount // 2 * 2:2]
    room = jnp.minimum(sizes[giver] - 1, limit - sizes[taker]) // 2
    room = jnp.where((giver == order[0]) | (taker == order[0]) | (sizes[taker] == 0), 0, jnp.maximum(room, 0))
    shifted = jax.random.randint(jax.random.fold_in(own, 4), (amount // 2,), 0, 1 << 20) % (room + 1)
    sizes = sizes.at[giver].add(-shifted).at[taker].add(shifted)
    items = jnp.searchsorted(jnp.cumsum(sizes), jnp.arange(rows * top), side="right").astype(jnp.int32)
    grid = items.reshape(top, rows).T
    grid = grid[jax.random.permutation(jax.random.fold_in(own, 1), rows)]
    rotation = jax.random.randint(jax.random.fold_in(own, 2), (rows, 1), 0, top)
    return jnp.take_along_axis(grid, (jnp.arange(top)[None, :] + rotation) % top, axis=1)


def load_shares(number_of, total, limit, lean, full):
    weights = [(1 << 20) // math.isqrt(rank ** lean) + 1 for rank in range(1, number_of + 1)]
    largest = limit if full else min(limit, max(-(-total // number_of), total * weights[0] // sum(weights)))
    least = 1 if total - largest >= number_of - 1 else 0
    holding, rest = [largest] + [least] * (number_of - 1), total - largest - least * (number_of - 1)
    while rest > 0:
        movable = [i for i in range(1, number_of) if holding[i] < largest] or [i for i in range(1, number_of) if holding[i] < limit]
        whole, budget = sum([weights[i] for i in movable]), rest
        for i in movable:
            addition = min(limit - holding[i], max(1, budget * weights[i] // whole), rest)
            holding[i] = holding[i] + addition
            rest = rest - addition
    return np.array(holding)


def scatter_about(key, extent, scale, bound, cuts=(), held_as=jnp.bfloat16):
    array = jax.random.normal(key, extent, jnp.float32) * scale
    if len(cuts) > 0:
        array = block_levels(key, extent, cuts, -0.22, 0.18) * array
    return jnp.clip(array, min=-bound, max=bound).astype(held_as)


def setup_inputs(seed: int = 0) -> dict:
    keys = jax.random.split(jax.random.key(seed), 18)
    hidden_in = draw_hidden_in(jax.random.fold_in(keys[17], 71), 0)
    new_lengths = jax.vmap(lambda own: uneven_parts(own, REQ, ROWS, NEW_MOST, 2))(jax.random.split(keys[1], N_REP)).reshape((N_REP, REQ)).astype(jnp.int32)
    prefix_lengths = jax.vmap(lambda own: uneven_parts(own, REQ, CACHE_ROWS, PREF_MOST, 2))(jax.random.split(keys[2], N_REP)).reshape((N_REP, REQ)).astype(jnp.int32)
    cache_keys = scatter_about(keys[3], (N_REP * CACHE_ROWS, D), 1.0, 6.0, ((0, 32), (1, 4)))
    cache_values = scatter_about(keys[4], (N_REP * CACHE_ROWS, D), 1.0, 6.0, ((0, 32), (1, 4)))
    attn_gain = jnp.clip(1.0 + 0.18 * jax.random.normal(keys[5], (D,), jnp.float32), 0.1, 1.9)
    w_qkv = draw_w_qkv(jax.random.fold_in(keys[17], 71), 0)
    norm_gains = draw_norm_gains(jax.random.fold_in(keys[17], 71), 0)
    w_out = scatter_about(keys[8], (D, D), D ** -0.5, 0.125, ((0, 4),))
    moe_gain = jnp.clip(1.0 + 0.18 * jax.random.normal(keys[9], (D,), jnp.float32), 0.1, 1.9)
    expert_ids_keys = jax.random.split(jax.random.fold_in(keys[10], 1), TOKENS // QROWS)
    expert_ids_turns = jax.random.permutation(jax.random.fold_in(keys[10], 3), TOKENS // QROWS)
    expert_ids = jax.vmap(lambda own, number: deal_out(jax.random.fold_in(keys[10], 2), own, number, QROWS, EXPERTS, TOP, CAPQ, 2))(expert_ids_keys, expert_ids_turns).reshape((TOKENS, TOP))
    expert_weights = jnp.clip(jnp.exp(math.log(0.5) - 2.3025851 * jax.random.uniform(keys[11], (TOKENS, TOP), jnp.float32) ** block_levels(keys[11], (TOKENS, TOP), ((0, 32),), -0.2, 0.2)), 0.05, 0.5)
    w_gate_up = scatter_about(keys[12], (EXPERTS, D, 2, FF), D ** -0.5, 0.125, ((0, 32), (3, 4)))
    w_down = scatter_about(keys[13], (EXPERTS, FF, D), FF ** -0.5, 0.1875, ((0, 32), (1, 4)))
    next_gain = jnp.clip(1.0 + 0.18 * jax.random.normal(keys[14], (D,), jnp.float32), 0.1, 1.9)
    next_qkv = draw_next_qkv(jax.random.fold_in(keys[17], 71), 0)
    next_norm_gains = jnp.clip(1.0 + 0.18 * jax.random.normal(keys[16], (2, D), jnp.float32), 0.1, 1.9)
    return dict(hidden_in=hidden_in, new_lengths=new_lengths, prefix_lengths=prefix_lengths, cache_keys=cache_keys, cache_values=cache_values, attn_gain=attn_gain, w_qkv=w_qkv, norm_gains=norm_gains, w_out=w_out, moe_gain=moe_gain, expert_ids=expert_ids, expert_weights=expert_weights, w_gate_up=w_gate_up, w_down=w_down, next_gain=next_gain, next_qkv=next_qkv, next_norm_gains=next_norm_gains)


eps_norm = 1e-05
eps_head = 1e-06
rope_base = 10000.0

def rms_scale(inputs, gain):
    inputs = inputs.astype(jnp.float32)
    scaled = inputs * lax.rsqrt(lax.optimization_barrier(jnp.mean(inputs * inputs, axis=-1, keepdims=True)) + eps_norm)
    return (scaled * gain).astype(jnp.bfloat16)

def request_tables(new_lengths, prefix_lengths, row_count, cache_count):
    new_end = jnp.cumsum(new_lengths, dtype=jnp.int32)
    cache_end = jnp.cumsum(prefix_lengths, dtype=jnp.int32)
    token_index = jnp.arange(row_count, dtype=jnp.int32)
    cache_index = jnp.arange(cache_count, dtype=jnp.int32)
    token_request = lax.optimization_barrier(jnp.sum((token_index[:, None] >= new_end[None, :]).astype(jnp.int32), axis=1, dtype=jnp.int32))
    cache_request = lax.optimization_barrier(jnp.sum((cache_index[:, None] >= cache_end[None, :]).astype(jnp.int32), axis=1, dtype=jnp.int32))
    requests = new_lengths.shape[0]
    selector = token_request[:, None] == jnp.arange(requests, dtype=jnp.int32)[None, :]
    new_start = new_end - new_lengths
    offset = token_index - lax.optimization_barrier(jnp.sum(jnp.where(selector, new_start[None, :], 0), axis=1, dtype=jnp.int32))
    position = offset + lax.optimization_barrier(jnp.sum(jnp.where(selector, prefix_lengths[None, :], 0), axis=1, dtype=jnp.int32))
    return (token_request, cache_request, position.astype(jnp.int32))

def project_heads(normed, weight, gains, position, head_size):
    row_count = normed.shape[0]
    proj_width = weight.shape[2]
    projected = jnp.dot(normed, weight.reshape(weight.shape[0], 3 * proj_width), preferred_element_type=jnp.float32)
    projected = projected.reshape(row_count, 3, proj_width)
    head_count = proj_width // head_size
    half_size = head_size // 2
    frequency = rope_base ** (-jnp.arange(half_size, dtype=jnp.float32) * 2.0 / head_size)
    angles = position.astype(jnp.float32)[:, None] * frequency[None, :]
    cosine = jnp.cos(angles)[:, None, :]
    sine_table = jnp.sin(angles)[:, None, :]
    outputs = []
    for member in range(2):
        member_rows = projected[:, member, :]
        member_rows = member_rows * lax.rsqrt(lax.optimization_barrier(jnp.mean(member_rows * member_rows, axis=-1, keepdims=True)) + eps_head)
        portion = (member_rows * gains[member][None, :]).reshape(row_count, head_count, head_size)
        lower_half = portion[..., :half_size]
        upper_half = portion[..., half_size:]
        turned = jnp.concatenate([lower_half * cosine - upper_half * sine_table, upper_half * cosine + lower_half * sine_table], axis=-1)
        outputs.append(turned.reshape(row_count, proj_width).astype(jnp.bfloat16))
    outputs.append(projected[:, 2, :].astype(jnp.bfloat16))
    return jnp.stack(outputs, axis=1)

def attend(qkv, key_cache, value_cache, token_request, cache_request, head_size):
    row_count = qkv.shape[0]
    proj_width = qkv.shape[2]
    head_count = proj_width // head_size
    queries = qkv[:, 0, :].reshape(row_count, head_count, head_size).astype(jnp.float32)
    key_rows = jnp.concatenate([key_cache, qkv[:, 1, :]], axis=0).reshape(-1, head_count, head_size).astype(jnp.float32)
    value_rows = jnp.concatenate([value_cache, qkv[:, 2, :]], axis=0).reshape(-1, head_count, head_size).astype(jnp.float32)
    scores = jnp.einsum('qhd,khd->hqk', queries, key_rows) / math.sqrt(head_size)
    token_index = jnp.arange(row_count, dtype=jnp.int32)
    cache_ok = cache_request[None, :] == token_request[:, None]
    new_ok = (token_request[None, :] == token_request[:, None]) & (token_index[None, :] <= token_index[:, None])
    allowed = jnp.concatenate([cache_ok, new_ok], axis=1)
    scores = jnp.where(allowed[None], scores, -1e+30)
    row_max = lax.optimization_barrier(jnp.max(scores, axis=-1, keepdims=True))
    weights = jnp.exp(scores - row_max)
    weights = (weights / lax.optimization_barrier(jnp.sum(weights, axis=-1, keepdims=True))).astype(jnp.bfloat16)
    context = jnp.einsum('hqk,khd->qhd', weights.astype(jnp.float32), value_rows)
    return context.reshape(row_count, proj_width).astype(jnp.bfloat16)

def slot_ranks(expert_rows, expert_count):
    onehot = (expert_rows[:, :, None] == jnp.arange(expert_count, dtype=jnp.int32)[None, None, :]).astype(jnp.int32)
    before = jnp.cumsum(onehot, axis=1, dtype=jnp.int32) - onehot
    return lax.optimization_barrier(jnp.sum(before * onehot, axis=2, dtype=jnp.int32))

def reference(hidden_in, new_lengths, prefix_lengths, cache_keys, cache_values, attn_gain, w_qkv, norm_gains, w_out, moe_gain, expert_ids, expert_weights, w_gate_up, w_down, next_gain, next_qkv, next_norm_gains):
    hidden_rep = hidden_in.reshape(N_REP, ROWS, D)
    keys_rep = cache_keys.reshape(N_REP, CACHE_ROWS, D)
    values_rep = cache_values.reshape(N_REP, CACHE_ROWS, D)

    def one_replica(members):
        hidden, lengths, prefixes, key_cache, value_cache = members
        token_request, cache_request, position = request_tables(lengths, prefixes, ROWS, CACHE_ROWS)
        normed = rms_scale(hidden, attn_gain)
        qkv = project_heads(normed, w_qkv, norm_gains, position, HD)
        context = attend(qkv, key_cache, value_cache, token_request, cache_request, HD)
        return (context, position)
    context, position = lax.map(one_replica, (hidden_rep, new_lengths, prefix_lengths, keys_rep, values_rep))
    context = context.reshape(TOKENS, D)
    position = position.reshape(TOKENS)
    attn_out = jnp.dot(context, w_out, preferred_element_type=jnp.float32)
    mid_stream = (hidden_in.astype(jnp.float32) + attn_out).astype(jnp.bfloat16)
    moe_input = rms_scale(mid_stream, moe_gain)
    blocks = TOKENS // QROWS
    rank_of = slot_ranks(expert_ids.reshape(blocks, QROWS * TOP), EXPERTS).reshape(-1)
    ids_flat = expert_ids.reshape(-1)
    entry = jnp.arange(TOKENS * TOP, dtype=jnp.int32)
    block_of = entry // (QROWS * TOP)
    per_expert = blocks * CAPQ
    slot_of = ids_flat * per_expert + block_of * CAPQ + rank_of
    slot_table = jnp.full((EXPERTS * per_expert,), TOKENS, jnp.int32).at[slot_of].set(entry // TOP)
    weight_table = jnp.zeros((EXPERTS * per_expert,), jnp.float32).at[slot_of].set(expert_weights.reshape(-1))
    padded = jnp.concatenate([moe_input, jnp.zeros((1, D), jnp.bfloat16)], axis=0)

    def one_expert(running, members):
        rows_idx, row_weights, gate_up, down_proj = members
        gathered = padded[rows_idx]
        gate_up_out = jnp.dot(gathered, gate_up.reshape(D, 2 * FF), preferred_element_type=jnp.float32)
        activated = (jax.nn.silu(gate_up_out[:, :FF]) * gate_up_out[:, FF:]).astype(jnp.bfloat16)
        contrib = jnp.zeros((rows_idx.shape[0], D), jnp.float32)
        for quarter in range(N_TP):
            portion = jnp.dot(activated[:, quarter * FF_TP:(quarter + 1) * FF_TP], down_proj[quarter * FF_TP:(quarter + 1) * FF_TP], preferred_element_type=jnp.float32).astype(jnp.bfloat16)
            contrib = contrib + portion.astype(jnp.float32)
        running = running.at[rows_idx].add(contrib * row_weights[:, None])
        return (running, None)
    running, _ = lax.scan(one_expert, jnp.zeros((TOKENS + 1, D), jnp.float32), (slot_table.reshape(EXPERTS, per_expert), weight_table.reshape(EXPERTS, per_expert), w_gate_up, w_down))
    moe_out = running[:TOKENS]
    hidden_out = (mid_stream.astype(jnp.float32) + moe_out).astype(jnp.bfloat16)
    next_input = rms_scale(hidden_out, next_gain)
    next_qkv_out = project_heads(next_input, next_qkv, next_norm_gains, position, HD)
    return (hidden_out, next_qkv_out)
```

```python
import functools
import math

import jax
import jax.numpy as jnp
from jax import lax
from jax.experimental import pallas as pl
from jax.experimental.pallas import tpu as pltpu
from jax.sharding import PartitionSpec as P

HD = 128
MESH = pl.DeviceIdType.MESH
F32 = jnp.float32
BF16 = jnp.bfloat16

eps_norm = 1e-05
eps_head = 1e-06
rope_base = 10000.0

ROWS = 128
D = 2048
Q = 32
AUX = 128
DG = D + AUX
NE = 64
CAP = 24
GATHER_PARTS = ((0, 768), (768, 768), (1536, 640))
REDUCE_PARTS = ((0, 768), (768, 640), (1408, 640))
ORDERS = ((1, 2, 0), (2, 0, 1), (0, 1, 2))
VMEM_LIMIT = 60 * 1024 * 1024


def place():
    rep = lax.axis_index("rep")
    return (rep // 8, (rep // 2) % 4, lax.axis_index("tp")), rep % 2


def device(coords, core):
    return (coords[0] * 8 + coords[1] * 2 + core, coords[2])


def moved(coords, axis, step):
    out = list(coords)
    out[axis] = (coords[axis] + step) % 4
    return tuple(out)


def greet(coords, core):
    barrier = pltpu.get_barrier_semaphore()
    peers = [device(coords, 1 - core), device(moved(coords, 2, 2), core)]
    for axis in range(3):
        for step in (1, 3):
            peers.append(device(moved(coords, axis, step), core))
    for peer in peers:
        pl.semaphore_signal(barrier, inc=1, device_id=peer, device_id_type=MESH)
    pl.semaphore_wait(barrier, len(peers))


def window(coords, axes, axis=None, value=None, rows=(0, Q), cols=(0, D)):
    index = []
    for a in range(3):
        if a in axes:
            index.append(pl.ds(0, 4))
        elif a == axis:
            index.append(value)
        else:
            index.append(coords[a])
    return tuple(index) + (pl.ds(rows[0], rows[1]), pl.ds(cols[0], cols[1]))


LO, HI, ALL = (0, 16), (16, 16), (0, Q)


def gather_kernel(part_ref, hidden_ref, gain_ref, aux_ref, g_ref, mid_ref,
                  inbox, own, tp_send, tp_recv, send, recv, sib_send, sib_recv, local_sem):
    coords, core = place()
    y = coords[2]
    greet(coords, core)
    tp_copies = []
    for k in range(1, 4):
        peer = (y + k) % 4
        copy = pltpu.make_async_remote_copy(
            src_ref=part_ref.at[pl.ds(pl.multiple_of(peer * Q, Q), Q), :],
            dst_ref=inbox.at[k - 1],
            send_sem=tp_send.at[k - 1],
            recv_sem=tp_recv.at[k - 1],
            device_id=device(moved(coords, 2, k), core),
            device_id_type=MESH,
        )
        copy.start()
        tp_copies.append(copy)
    rows = pl.ds(pl.multiple_of(y * Q, Q), Q)
    total = part_ref[rows, :].astype(F32)
    for k in range(3):
        tp_copies[k].wait_recv()
    for k in range(3):
        total = total + inbox[k].astype(F32)
    mid = (hidden_ref[rows, :].astype(F32) + total).astype(BF16)
    mid_ref[...] = mid
    wide = mid.astype(F32)
    scale = lax.rsqrt(jnp.mean(wide * wide, axis=-1, keepdims=True) + eps_norm)
    own[:, pl.ds(0, D)] = (wide * scale * gain_ref[...]).astype(BF16)
    own[:, pl.ds(D, AUX)] = aux_ref[rows, :]
    pending = list(tp_copies)
    here = pltpu.make_async_copy(own, g_ref.at[(core,) + coords], local_sem)
    here.start()

    def push(src, index, send_sem, recv_sem, peer):
        copy = pltpu.make_async_remote_copy(
            src_ref=src, dst_ref=g_ref.at[(core,) + index], send_sem=send_sem, recv_sem=recv_sem,
            device_id=peer, device_id_type=MESH,
        )
        copy.start()
        pending.append(copy)
        return copy

    sibling = device(coords, 1 - core)
    arrivals = []

    def forward(index, p, slot):
        arrivals.append(push(g_ref.at[(core,) + index], index, sib_send.at[p, slot], sib_recv.at[p, slot], sibling))

    for phase in range(3):
        steps = []
        for p in range(3):
            axis = ORDERS[p][phase]
            axes = ORDERS[p][:phase]
            cols = GATHER_PARTS[p]
            a = coords[axis]
            index = window(coords, axes, axis, a, ALL, cols)
            src = own.at[:, pl.ds(*cols)] if phase == 0 else g_ref.at[(core,) + index]
            right = device(moved(coords, axis, 1), core)
            left = device(moved(coords, axis, 3), core)
            to_right = push(src, index, send.at[p, phase, 0], recv.at[p, phase, 0], right)
            to_left = push(src, index, send.at[p, phase, 1], recv.at[p, phase, 1], left)
            steps.append((axis, axes, cols, a, right, left, to_right, to_left))
        if phase == 0:
            for p in range(3):
                cols = GATHER_PARTS[p]
                index = window(coords, (), None, None, ALL, cols)
                arrivals.append(push(own.at[:, pl.ds(*cols)], index, sib_send.at[p, 0], sib_recv.at[p, 0], sibling))
        ends = []
        for p in range(3):
            axis, axes, cols, a, right, left, to_right, to_left = steps[p]
            to_right.wait_recv()
            low = window(coords, axes, axis, (a + 3) % 4, LO, cols)
            far_low = push(g_ref.at[(core,) + low], low, send.at[p, phase, 2], recv.at[p, phase, 2], right)
            to_left.wait_recv()
            high = window(coords, axes, axis, (a + 1) % 4, HI, cols)
            far_high = push(g_ref.at[(core,) + high], high, send.at[p, phase, 3], recv.at[p, phase, 3], left)
            forward(window(coords, axes, axis, (a + 3) % 4, ALL, cols), p, 1 + 4 * phase)
            forward(window(coords, axes, axis, (a + 1) % 4, ALL, cols), p, 2 + 4 * phase)
            ends.append((far_low, far_high))
        if phase == 0:
            here.wait()
        for p in range(3):
            axis, axes, cols, a = steps[p][:4]
            ends[p][0].wait_recv()
            forward(window(coords, axes, axis, (a + 2) % 4, LO, cols), p, 3 + 4 * phase)
            ends[p][1].wait_recv()
            forward(window(coords, axes, axis, (a + 2) % 4, HI, cols), p, 4 + 4 * phase)
    for copy in arrivals:
        copy.wait_recv()
    for copy in pending:
        copy.wait_send()


def gather_rows(part, hidden, gain, aux):
    return pl.pallas_call(
        gather_kernel,
        name="dispatch_rows",
        out_shape=(
            jax.ShapeDtypeStruct((2, 4, 4, 4, Q, DG), BF16),
            jax.ShapeDtypeStruct((Q, D), BF16),
        ),
        in_specs=[pl.BlockSpec(memory_space=pltpu.VMEM)] * 4,
        out_specs=(pl.BlockSpec(memory_space=pltpu.HBM), pl.BlockSpec(memory_space=pltpu.VMEM)),
        scratch_shapes=[
            pltpu.VMEM((3, Q, D), BF16),
            pltpu.VMEM((Q, DG), BF16),
            pltpu.SemaphoreType.DMA((3,)),
            pltpu.SemaphoreType.DMA((3,)),
            pltpu.SemaphoreType.DMA((3, 3, 4)),
            pltpu.SemaphoreType.DMA((3, 3, 4)),
            pltpu.SemaphoreType.DMA((3, 13)),
            pltpu.SemaphoreType.DMA((3, 13)),
            pltpu.SemaphoreType.DMA,
        ],
        compiler_params=pltpu.CompilerParams(
            collective_id=0, has_side_effects=True, vmem_limit_bytes=VMEM_LIMIT
        ),
    )(part, hidden, gain, aux)


def expert_kernel(g_ref, gu_ref, down_ref, p_ref, xs, ys, hot, scale):
    rep = lax.axis_index("rep")
    groups = g_ref.shape[0] // 256
    width = 2 * CAP
    lane = lax.broadcasted_iota(jnp.int32, (256, 128), 1)
    row = lax.broadcasted_iota(jnp.int32, (256, 1), 0)
    second = (row >= ROWS).astype(jnp.int32)
    tri_r = lax.broadcasted_iota(jnp.int32, (256, 256), 0)
    tri_c = lax.broadcasted_iota(jnp.int32, (256, 256), 1)
    earlier = jnp.where((tri_c < tri_r) & ((tri_c >= ROWS) == (tri_r >= ROWS)), 1.0, 0.0).astype(BF16)
    slot_lane = lax.broadcasted_iota(jnp.int32, (width, 128), 1)

    def collect(i, carry):
        rows = pl.ds(pl.multiple_of(i * 256, 256), 256)
        weights = g_ref[rows, pl.ds(D, AUX)].astype(F32)
        chosen = jnp.where(weights > 0, 1.0, 0.0)
        ranks = jnp.dot(earlier, chosen.astype(BF16), preferred_element_type=F32)
        match = jnp.zeros((256, 128), F32)
        for j in range(2):
            mine = lane == 2 * rep + j
            picked = jnp.sum(jnp.where(mine, chosen, 0.0), axis=1, keepdims=True)
            rank = jnp.sum(jnp.where(mine, ranks, 0.0), axis=1, keepdims=True).astype(jnp.int32)
            slot = jnp.where(picked > 0, rank + second * CAP + j * width, -1)
            match = match + jnp.where(lane == slot, 1.0, 0.0)
        hot[rows, :] = match.astype(BF16)
        select = match.T.astype(BF16)
        got = jnp.dot(select, g_ref[rows, :], preferred_element_type=F32)
        for j in range(2):
            out_rows = pl.ds(pl.multiple_of(i * width, 16), width)
            block = got[j * width:(j + 1) * width]
            xs[j, out_rows, :] = block[:, :D].astype(BF16)
            wide = block[:, D:]
            mine = (slot_lane == 2 * rep + j) | (slot_lane == 2 * rep + j + NE)
            scale[j, out_rows, :] = jnp.broadcast_to(
                jnp.sum(jnp.where(mine, wide, 0.0), axis=1, keepdims=True), (width, 128))
        return carry

    lax.fori_loop(0, groups, collect, 0)
    for j in range(2):
        x = xs[j]
        gate = jnp.dot(x, gu_ref[j, 0], preferred_element_type=F32)
        up = jnp.dot(x, gu_ref[j, 1], preferred_element_type=F32)
        act = gate / (1.0 + jnp.exp(-gate)) * up
        act = (act * scale[j][:, :1]).astype(BF16)
        ys[j] = jnp.dot(act, down_ref[j], preferred_element_type=F32).astype(BF16)

    def spread(i, carry):
        rows = pl.ds(pl.multiple_of(i * 256, 256), 256)
        in_rows = pl.ds(pl.multiple_of(i * width, 16), width)
        both = jnp.concatenate([ys[0, in_rows, :], ys[1, in_rows, :]], axis=0)
        p_ref[rows, :] = jnp.dot(
            hot[rows, pl.ds(0, 128)][:, :2 * width], both, preferred_element_type=F32).astype(BF16)
        return carry

    lax.fori_loop(0, groups, spread, 0)


def expert_rows(g, gate_up, down):
    step = 1024
    slots = step // 256 * 2 * CAP
    return pl.pallas_call(
        expert_kernel,
        name="experts",
        grid=(g.shape[0] // step,),
        out_shape=jax.ShapeDtypeStruct((g.shape[0], D), BF16),
        in_specs=[
            pl.BlockSpec((step, DG), lambda i: (i, 0)),
            pl.BlockSpec(memory_space=pltpu.VMEM),
            pl.BlockSpec(memory_space=pltpu.VMEM),
        ],
        out_specs=pl.BlockSpec((step, D), lambda i: (i, 0)),
        scratch_shapes=[
            pltpu.VMEM((2, slots, D), BF16),
            pltpu.VMEM((2, slots, D), BF16),
            pltpu.VMEM((step, 128), BF16),
            pltpu.VMEM((2, slots, 128), F32),
        ],
        compiler_params=pltpu.CompilerParams(vmem_limit_bytes=VMEM_LIMIT),
    )(g, gate_up, down)


def reduce_kernel(p_ref, mid_ref, hidden_ref,
                  q, sib, f0, f1, f2, h0, h1, h2, out,
                  load_sem, sib_send, sib_recv, send, recv, tp_send, tp_recv):
    coords, core = place()
    y = coords[2]
    greet(coords, core)
    sibling = device(coords, 1 - core)
    fulls, halves = (f0, f1, f2), (h0, h1, h2)
    loads, exchanges, pending = {}, {}, []
    for n in range(4):
        for p in range(3):
            axis = ORDERS[p][2]
            axes = ORDERS[p][:2]
            value = (coords[axis] + (2, 1, 3, 0)[n]) % 4
            index = window(coords, axes, axis, value, ALL, REDUCE_PARTS[p])
            copy = pltpu.make_async_remote_copy(
                src_ref=p_ref.at[(1 - core,) + index], dst_ref=sib.at[index],
                send_sem=sib_send.at[p, n], recv_sem=sib_recv.at[p, n],
                device_id=sibling, device_id_type=MESH)
            copy.start()
            exchanges[p, n] = copy
            pending.append(copy)
            load = pltpu.make_async_copy(p_ref.at[(core,) + index], q.at[index], load_sem.at[p, n])
            load.start()
            loads[p, n] = load

    def sweep(phase, p, axis, value, body):
        axes = ORDERS[p][:2 - phase]
        free = sorted(axes)

        def one(i):
            inner = (i // 4, i % 4) if len(free) == 2 else ((i,) if len(free) == 1 else ())
            at = [coords[a] for a in range(3)]
            at[axis] = value
            for a, v in zip(free, inner):
                at[a] = v
            body(tuple(at), inner)

        count = 4 ** len(free)
        if count == 1:
            one(0)
        else:
            def step(i, carry):
                one(i)
                return carry
            lax.fori_loop(0, count, step, 0)

    def add_sibling(p, n):
        axis = ORDERS[p][2]
        cols = REDUCE_PARTS[p]
        value = (coords[axis] + (2, 1, 3, 0)[n]) % 4
        loads[p, n].wait()
        exchanges[p, n].wait_recv()

        def body(at, inner):
            spot = at + (slice(None), pl.ds(*cols))
            q[spot] = q[spot] + sib[spot]
        sweep(0, p, axis, value, body)

    def push(phase, p, slot, src_index, dst, peer):
        copy = pltpu.make_async_remote_copy(
            src_ref=q.at[src_index], dst_ref=dst,
            send_sem=send.at[p, phase, slot], recv_sem=recv.at[p, phase, slot],
            device_id=peer, device_id_type=MESH)
        copy.start()
        pending.append(copy)
        return copy

    def band(ref, p, side, axes, rows):
        width = REDUCE_PARTS[p][1]
        lead = (p, side) + (slice(None),) * len(axes)
        return ref.at[lead + (pl.ds(*rows), pl.ds(0, width))]

    for phase in range(3):
        state = []
        for p in range(3):
            axis = ORDERS[p][2 - phase]
            axes = ORDERS[p][:2 - phase]
            cols = REDUCE_PARTS[p]
            a = coords[axis]
            right = device(moved(coords, axis, 1), core)
            left = device(moved(coords, axis, 3), core)
            full, half = fulls[phase], halves[phase]
            if phase == 0:
                add_sibling(p, 0)
            opposite = (a + 2) % 4
            first = push(phase, p, 0, window(coords, axes, axis, opposite, LO, cols), band(half, p, 0, axes, LO), right)
            second = push(phase, p, 1, window(coords, axes, axis, opposite, HI, cols), band(half, p, 1, axes, LO), left)
            state.append((axis, axes, cols, a, right, left, full, half, first, second))
        tails = []
        for p in range(3):
            axis, axes, cols, a, right, left, full, half, first, second = state[p]
            if phase == 0:
                add_sibling(p, 1)
            t0 = push(phase, p, 2, window(coords, axes, axis, (a + 1) % 4, HI, cols), band(full, p, 0, axes, HI), right)
            if phase == 0:
                add_sibling(p, 2)
            t1 = push(phase, p, 3, window(coords, axes, axis, (a + 3) % 4, LO, cols), band(full, p, 1, axes, LO), left)
            tails.append([t0, t1])
        for p in range(3):
            axis, axes, cols, a, right, left, full, half, first, second = state[p]
            for side, came, value, rows, peer, slot in (
                (0, first, (a + 1) % 4, LO, right, 4), (1, second, (a + 3) % 4, HI, left, 5),
            ):
                came.wait_recv()

                def body(at, inner, side=side, rows=rows):
                    spot = at + (pl.ds(*rows), pl.ds(*cols))
                    q[spot] = q[spot] + half[(p, side) + inner + (slice(None), pl.ds(0, cols[1]))]
                sweep(phase, p, axis, value, body)
                tails[p].append(push(phase, p, slot, window(coords, axes, axis, value, rows, cols),
                                     band(full, p, side, axes, rows), peer))
        for p in range(3):
            axis, axes, cols, a, right, left, full, half, first, second = state[p]
            if phase == 0:
                add_sibling(p, 3)
            for copy in tails[p]:
                copy.wait_recv()

            def body(at, inner):
                spot = at + (slice(None), pl.ds(*cols))
                one = full[(p, 0) + inner + (slice(None), pl.ds(0, cols[1]))].astype(F32)
                two = full[(p, 1) + inner + (slice(None), pl.ds(0, cols[1]))].astype(F32)
                total = q[spot].astype(F32) + one + two
                if phase == 2:
                    out[y, :, pl.ds(*cols)] = (mid_ref[:, pl.ds(*cols)].astype(F32) + total).astype(BF16)
                else:
                    q[spot] = total.astype(BF16)
            sweep(phase, p, axis, a, body)
    last = []
    for k in range(1, 4):
        copy = pltpu.make_async_remote_copy(
            src_ref=out.at[y], dst_ref=out.at[y], send_sem=tp_send.at[k - 1], recv_sem=tp_recv.at[k - 1],
            device_id=device(moved(coords, 2, k), core), device_id_type=MESH)
        copy.start()
        last.append(copy)
    for copy in last:
        copy.wait()
    for copy in pending:
        copy.wait_send()
    for b in range(4):
        hidden_ref[pl.ds(b * Q, Q), :] = out[b]


def reduce_rows(partial, mid):
    width = max(w for _, w in REDUCE_PARTS)
    return pl.pallas_call(
        reduce_kernel,
        name="combine_rows",
        out_shape=jax.ShapeDtypeStruct((ROWS, D), BF16),
        in_specs=[pl.BlockSpec(memory_space=pltpu.HBM), pl.BlockSpec(memory_space=pltpu.VMEM)],
        out_specs=pl.BlockSpec(memory_space=pltpu.VMEM),
        scratch_shapes=[
            pltpu.VMEM((4, 4, 4, Q, D), BF16),
            pltpu.VMEM((4, 4, 4, Q, D), BF16),
            pltpu.VMEM((3, 2, 4, 4, Q, width), BF16),
            pltpu.VMEM((3, 2, 4, Q, width), BF16),
            pltpu.VMEM((3, 2, Q, width), BF16),
            pltpu.VMEM((3, 2, 4, 4, Q // 2, width), BF16),
            pltpu.VMEM((3, 2, 4, Q // 2, width), BF16),
            pltpu.VMEM((3, 2, Q // 2, width), BF16),
            pltpu.VMEM((4, Q, D), BF16),
            pltpu.SemaphoreType.DMA((3, 4)),
            pltpu.SemaphoreType.DMA((3, 4)),
            pltpu.SemaphoreType.DMA((3, 4)),
            pltpu.SemaphoreType.DMA((3, 3, 6)),
            pltpu.SemaphoreType.DMA((3, 3, 6)),
            pltpu.SemaphoreType.DMA((3,)),
            pltpu.SemaphoreType.DMA((3,)),
        ],
        compiler_params=pltpu.CompilerParams(
            collective_id=1, has_side_effects=True, vmem_limit_bytes=VMEM_LIMIT
        ),
    )(partial, mid)


def rms_scale(inputs, gain):
    inputs = inputs.astype(F32)
    scaled = inputs * lax.rsqrt(jnp.mean(inputs * inputs, axis=-1, keepdims=True) + eps_norm)
    return (scaled * gain).astype(BF16)


def request_tables(new_lengths, prefix_lengths, row_count, cache_count):
    new_end = jnp.cumsum(new_lengths, dtype=jnp.int32)
    cache_end = jnp.cumsum(prefix_lengths, dtype=jnp.int32)
    token_index = jnp.arange(row_count, dtype=jnp.int32)
    cache_index = jnp.arange(cache_count, dtype=jnp.int32)
    token_request = jnp.sum(
        (token_index[:, None] >= new_end[None, :]).astype(jnp.int32), axis=1, dtype=jnp.int32
    )
    cache_request = jnp.sum(
        (cache_index[:, None] >= cache_end[None, :]).astype(jnp.int32), axis=1, dtype=jnp.int32
    )
    requests = new_lengths.shape[0]
    selector = token_request[:, None] == jnp.arange(requests, dtype=jnp.int32)[None, :]
    new_start = new_end - new_lengths
    offset = token_index - jnp.sum(
        jnp.where(selector, new_start[None, :], 0), axis=1, dtype=jnp.int32
    )
    position = offset + jnp.sum(
        jnp.where(selector, prefix_lengths[None, :], 0), axis=1, dtype=jnp.int32
    )
    return (token_request, cache_request, position)


def project_heads(normed, weight, gains, position, head_size):
    row_count = normed.shape[0]
    proj_width = weight.shape[2]
    full_width = proj_width * lax.axis_size("tp")
    by_member = jnp.transpose(weight, (1, 0, 2))
    projected = [
        jnp.dot(normed, by_member[m], preferred_element_type=F32) for m in range(3)
    ]
    squares = jnp.stack([jnp.sum(projected[m] * projected[m], axis=1) for m in range(2)], axis=1)
    totals = lax.psum(squares, "tp")
    inverse = lax.rsqrt(totals / full_width + eps_head)
    head_count = proj_width // head_size
    half_size = head_size // 2
    frequency = rope_base ** (-jnp.arange(half_size, dtype=F32) * 2.0 / head_size)
    angles = position.astype(F32)[:, None] * frequency[None, :]
    cosine = jnp.cos(angles)[:, None, :]
    sine_table = jnp.sin(angles)[:, None, :]
    outputs = []
    for member in range(2):
        member_rows = projected[member] * inverse[:, member : member + 1]
        portion = (member_rows * gains[member][None, :]).reshape(row_count, head_count, head_size)
        lower_half = portion[..., :half_size]
        upper_half = portion[..., half_size:]
        turned = jnp.concatenate(
            [
                lower_half * cosine - upper_half * sine_table,
                upper_half * cosine + lower_half * sine_table,
            ],
            axis=-1,
        )
        outputs.append(turned.reshape(row_count, proj_width).astype(BF16))
    outputs.append(projected[2].astype(BF16))
    return outputs


def attend(qkv, key_cache, value_cache, token_request, cache_request, head_size):
    row_count, proj_width = qkv[0].shape
    head_count = proj_width // head_size
    queries = qkv[0].reshape(row_count, head_count, head_size)
    key_rows = jnp.concatenate([key_cache, qkv[1]], axis=0).reshape(-1, head_count, head_size)
    value_rows = jnp.concatenate([value_cache, qkv[2]], axis=0).reshape(
        -1, head_count, head_size
    )
    scores = jnp.einsum(
        "qhd,khd->hqk", queries, key_rows, preferred_element_type=F32
    ) / math.sqrt(head_size)
    token_index = jnp.arange(row_count, dtype=jnp.int32)
    cache_ok = cache_request[None, :] == token_request[:, None]
    new_ok = (token_request[None, :] == token_request[:, None]) & (
        token_index[None, :] <= token_index[:, None]
    )
    allowed = jnp.concatenate([cache_ok, new_ok], axis=1)
    scores = jnp.where(allowed[None], scores, -1e30)
    row_max = jnp.max(scores, axis=-1, keepdims=True)
    weights = jnp.exp(scores - row_max)
    weights = (weights / jnp.sum(weights, axis=-1, keepdims=True)).astype(BF16)
    context = jnp.einsum("hqk,khd->qhd", weights, value_rows, preferred_element_type=F32)
    return context.reshape(row_count, proj_width).astype(BF16)


def weight_columns(expert_ids, expert_weights):
    experts = jnp.arange(NE, dtype=jnp.int32)[None, :]
    dense = jnp.zeros((expert_ids.shape[0], NE), F32)
    for k in range(expert_ids.shape[1]):
        dense = dense + jnp.where(expert_ids[:, k:k + 1] == experts, expert_weights[:, k:k + 1], 0.0)
    high = lax.reduce_precision(dense, 8, 7)
    return jnp.concatenate([high, dense - high], axis=1).astype(BF16)


def per_device(
    hidden_in,
    new_lengths,
    prefix_lengths,
    cache_keys,
    cache_values,
    attn_gain,
    w_qkv,
    norm_gains,
    w_out,
    moe_gain,
    expert_ids,
    expert_weights,
    w_gate_up,
    w_down,
    next_gain,
    next_qkv,
    next_norm_gains,
):
    row_count, model_width = hidden_in.shape
    cache_count = cache_keys.shape[0]
    token_request, cache_request, position = request_tables(
        new_lengths[0], prefix_lengths[0], row_count, cache_count
    )
    normed = rms_scale(hidden_in, attn_gain)
    qkv = project_heads(normed, w_qkv, norm_gains, position, HD)
    context = attend(qkv, cache_keys, cache_values, token_request, cache_request, HD)
    attn_part = jnp.dot(context, w_out, preferred_element_type=F32).astype(BF16)
    aux = weight_columns(expert_ids, expert_weights)
    gathered, mid = gather_rows(attn_part, hidden_in, moe_gain[None, :], aux)
    partial = expert_rows(
        gathered.reshape(-1, DG), jnp.transpose(w_gate_up, (0, 2, 1, 3)), w_down)
    hidden_out = reduce_rows(partial.reshape(2, 4, 4, 4, Q, D), mid)
    next_input = rms_scale(hidden_out, next_gain)
    next_out = project_heads(next_input, next_qkv, next_norm_gains, position, HD)
    return (hidden_out, jnp.stack(next_out, axis=1))


def solution(mesh):
    placed = (
        P("rep", None),
        P("rep", None),
        P("rep", None),
        P("rep", "tp"),
        P("rep", "tp"),
        P(),
        P(None, None, "tp"),
        P(None, "tp"),
        P("tp", None),
        P(),
        P("rep", None),
        P("rep", None),
        P("rep", None, None, "tp"),
        P("rep", "tp", None),
        P(),
        P(None, None, "tp"),
        P(None, "tp"),
    )
    return jax.shard_map(
        per_device,
        mesh=mesh,
        in_specs=placed,
        out_specs=(P("rep", None), P("rep", None, "tp")),
        check_vma=False,
    )
```

```python
import functools
import math

import jax
import jax.numpy as jnp
from jax import lax
from jax.experimental import pallas as pl
from jax.experimental.pallas import tpu as pltpu
from jax.sharding import PartitionSpec as P

HD = 128
MESH = pl.DeviceIdType.MESH
F32 = jnp.float32
BF16 = jnp.bfloat16

eps_norm = 1e-05
eps_head = 1e-06
rope_base = 10000.0

ROWS = 128
D = 2048
Q = 32
AUX = 128
HALF = D // 2
WIDE = HALF + AUX
NE = 64
CAP = 24
GATHER_PARTS = ((0, 384), (384, 384), (768, 384))
REDUCE_PARTS = ((0, 384), (384, 384), (768, 256))
ORDERS = ((1, 2, 0), (2, 0, 1), (0, 1, 2))
VMEM_LIMIT = 60 * 1024 * 1024


def place():
    rep = lax.axis_index("rep")
    return (rep // 8, (rep // 2) % 4, lax.axis_index("tp")), rep % 2


def device(coords, core):
    return (coords[0] * 8 + coords[1] * 2 + core, coords[2])


def moved(coords, axis, step):
    out = list(coords)
    out[axis] = (coords[axis] + step) % 4
    return tuple(out)


def greet(coords, core):
    barrier = pltpu.get_barrier_semaphore()
    peers = [device(coords, 1 - core)]
    for axis in range(3):
        for step in (1, 2, 3):
            peers.append(device(moved(coords, axis, step), core))
    for peer in peers:
        pl.semaphore_signal(barrier, inc=1, device_id=peer, device_id_type=MESH)
    pl.semaphore_wait(barrier, len(peers))


WHOLE = pl.ds(0, 4)
LO, HI, ALL = (0, 16), (16, 16), (0, Q)
WIDTH = 2 * CAP
SLOTS = 16 * CAP


def window(coords, at, rows, cols):
    index = tuple(at.get(axis, coords[axis]) for axis in range(3))
    return index + (pl.ds(*rows), pl.ds(*cols))


def moe_kernel(part_ref, hidden_ref, gain_ref, aux_ref, gu_hbm, down_hbm, out_ref, g_ref,
               inbox, own, mid, gu, down, gbuf, xs, ys, hot, scale, part, sib,
               near, far, mnear, mfar, first, result, other, out,
               tp_send, tp_recv, ag_send, ag_recv, share_send, share_recv, local_sem, load_sem, weight_sem,
               sib_send, sib_recv, rs_send, rs_recv, swap_send, swap_recv, end_send, end_recv):
    coords, core = place()
    rep = lax.axis_index("rep")
    y = coords[2]
    sibling = device(coords, 1 - core)
    pending = []
    fetch = [pltpu.make_async_copy(gu_hbm, gu, weight_sem.at[0]), pltpu.make_async_copy(down_hbm, down, weight_sem.at[1])]
    for copy in fetch:
        copy.start()
    greet(coords, core)

    def push(src, dst, send_sem, recv_sem, peer):
        copy = pltpu.make_async_remote_copy(
            src_ref=src, dst_ref=dst, send_sem=send_sem, recv_sem=recv_sem, device_id=peer, device_id_type=MESH)
        copy.start()
        pending.append(copy)
        return copy

    tp_copies = []
    for k in (2, 1, 3):
        peer = (y + k) % 4
        tp_copies.append(push(
            part_ref.at[pl.ds(pl.multiple_of(peer * Q, Q), Q), :], inbox.at[k - 1],
            tp_send.at[k - 1], tp_recv.at[k - 1], device(moved(coords, 2, k), core)))
    rows = pl.ds(pl.multiple_of(y * Q, Q), Q)
    total = part_ref[rows, :].astype(F32)
    for copy in tp_copies:
        copy.wait_recv()
    for k in range(3):
        total = total + inbox[k].astype(F32)
    stream = (hidden_ref[rows, :].astype(F32) + total).astype(BF16)
    mid[...] = stream
    wide = stream.astype(F32)
    inverse = lax.rsqrt(jnp.mean(wide * wide, axis=-1, keepdims=True) + eps_norm)
    normed = (wide * inverse * gain_ref[...]).astype(BF16)
    for h in range(2):
        own[2 + h, :, pl.ds(0, HALF)] = normed[:, h * HALF:(h + 1) * HALF]
        own[2 + h, :, pl.ds(HALF, AUX)] = aux_ref[rows, :]
    own[core] = own[2 + core]
    swap = push(own.at[2 + (1 - core)], own.at[core], swap_send.at[0], swap_recv.at[0], sibling)
    return_own = swap

    def gather(chunk):
        def at(index):
            return g_ref.at[(chunk, core) + index]

        arrivals = []

        def share(p, slot, index, src=None):
            arrivals.append(push(at(index) if src is None else src, at(index),
                                 share_send.at[chunk, p, slot], share_recv.at[chunk, p, slot], sibling))

        class Ring:
            def __init__(self, p, number, axis, where):
                self.p, self.base, self.axis, self.where = p, number * 4, axis, where
                self.a = coords[axis]
                self.right = device(moved(coords, axis, 1), core)
                self.left = device(moved(coords, axis, 3), core)
                self.ends = [self.push(0, self.index(0), self.right), self.push(1, self.index(0), self.left)]

            def index(self, step, rows=ALL):
                return window(coords, {**self.where, self.axis: (self.a + step) % 4}, rows, GATHER_PARTS[self.p])

            def push(self, k, index, peer):
                n = self.base + k
                return push(at(index), at(index), ag_send.at[chunk, self.p, n], ag_recv.at[chunk, self.p, n], peer)

            def near(self):
                for k, step, rows, peer in ((0, 3, LO, self.right), (1, 1, HI, self.left)):
                    self.ends[k].wait_recv()
                    self.ends.append(self.push(2 + k, self.index(step, rows), peer))

            def far(self):
                self.ends[2].wait_recv()
                self.ends[3].wait_recv()

        firsts = []
        for p in range(3):
            axis = ORDERS[p][0]
            index = window(coords, {}, ALL, GATHER_PARTS[p])
            src = own.at[chunk, :, pl.ds(*GATHER_PARTS[p])]
            firsts.append([
                push(src, at(index), ag_send.at[chunk, p, k - 1], ag_recv.at[chunk, p, k - 1],
                     device(moved(coords, axis, k), core))
                for k in (1, 3, 2)
            ])
        here = pltpu.make_async_copy(own.at[chunk], g_ref.at[(chunk, core) + coords], local_sem.at[chunk])
        here.start()
        yield
        here.wait()
        rings = []
        for p in range(3):
            for copy in firsts[p]:
                copy.wait_recv()
            rings.append(Ring(p, 1, ORDERS[p][1], {ORDERS[p][0]: WHOLE}))
        yield
        for ring in rings:
            ring.near()
        yield
        for p in range(3):
            one, two, three = ORDERS[p]
            rings[p].far()
            rings[p] = Ring(p, 2, three, {one: WHOLE, two: WHOLE})
            share(p, 0, rings[p].index(0))
        yield
        for p in range(3):
            rings[p].near()
            share(p, 1, rings[p].index(3))
            share(p, 2, rings[p].index(1))
        yield
        for p in range(3):
            rings[p].far()
            share(p, 3, rings[p].index(2))
        yield
        for copy in arrivals:
            copy.wait_recv()

    lane = lax.broadcasted_iota(jnp.int32, (256, 128), 1)
    second = (lax.broadcasted_iota(jnp.int32, (256, 1), 0) >= ROWS).astype(jnp.int32)
    slot_lane = lax.broadcasted_iota(jnp.int32, (WIDTH, 128), 1)

    def experts(chunk):
        def load(z):
            copies = [
                pltpu.make_async_copy(g_ref.at[chunk, h, z], gbuf.at[z % 2, h], load_sem.at[z % 2, h]) for h in range(2)
            ]
            for copy in copies:
                copy.start()
            return copies

        def collect(z, i):
            tri_r = lax.broadcasted_iota(jnp.int32, (256, 256), 0)
            tri_c = lax.broadcasted_iota(jnp.int32, (256, 256), 1)
            earlier = jnp.where((tri_c < tri_r) & ((tri_c >= ROWS) == (tri_r >= ROWS)), 1.0, 0.0).astype(BF16)
            blocks = pl.ds(2 * i, 2)
            low = gbuf[z % 2, 0, blocks].reshape(256, WIDE)
            high = gbuf[z % 2, 1, blocks].reshape(256, WIDE)[:, :HALF]
            chosen = jnp.where(low[:, HALF:].astype(F32) > 0, 1.0, 0.0)
            ranks = jnp.dot(earlier, chosen.astype(BF16), preferred_element_type=F32)
            match = jnp.zeros((256, 128), F32)
            for j in range(2):
                mine = lane == 2 * rep + j
                picked = jnp.sum(jnp.where(mine, chosen, 0.0), axis=1, keepdims=True)
                rank = jnp.sum(jnp.where(mine, ranks, 0.0), axis=1, keepdims=True).astype(jnp.int32)
                slot = jnp.where(picked > 0, rank + second * CAP + j * WIDTH, -1)
                match = match + jnp.where(lane == slot, 1.0, 0.0)
            hot[2 * z + i] = match.astype(BF16)
            select = match.T[:2 * WIDTH].astype(BF16)
            got_low = jnp.dot(select, low, preferred_element_type=F32)
            got_high = jnp.dot(select, high, preferred_element_type=F32)
            slots = pl.ds(pl.multiple_of((2 * z + i) * WIDTH, 16), WIDTH)
            for j in range(2):
                span = slice(j * WIDTH, (j + 1) * WIDTH)
                xs[j, slots, pl.ds(0, HALF)] = got_low[span, :HALF].astype(BF16)
                xs[j, slots, pl.ds(HALF, HALF)] = got_high[span].astype(BF16)
                mine = (slot_lane == 2 * rep + j) | (slot_lane == 2 * rep + j + NE)
                scale[j, slots, :] = jnp.broadcast_to(
                    jnp.sum(jnp.where(mine, got_low[span, HALF:], 0.0), axis=1, keepdims=True), (WIDTH, 128))

        def looped(body, z):
            def step(i, carry):
                body(z, i)
                return carry
            lax.fori_loop(0, 2, step, 0)

        def spread(z, i):
            slots = pl.ds(pl.multiple_of((2 * z + i) * WIDTH, 16), WIDTH)
            both = jnp.concatenate([ys[0, slots, :], ys[1, slots, :]], axis=0)
            back = jnp.dot(hot[2 * z + i][:, :2 * WIDTH], both, preferred_element_type=F32).astype(BF16)
            for h in range(2):
                part[chunk, h, z, pl.ds(2 * i, 2)] = back[:, h * HALF:(h + 1) * HALF].reshape(2, 4, Q, HALF)

        copies = load(0)
        for z in range(4):
            coming = load(z + 1) if z < 3 else None
            for copy in copies:
                copy.wait()
            looped(collect, z)
            copies = coming
            yield
        if chunk == 0:
            for copy in fetch:
                copy.wait()
        for j in range(2):
            x = xs[j]
            gate = jnp.dot(x, gu[j, 0], preferred_element_type=F32)
            up = jnp.dot(x, gu[j, 1], preferred_element_type=F32)
            act = gate / (1.0 + jnp.exp(-gate)) * up
            act = (act * scale[j][:, :1]).astype(BF16)
            ys[j] = jnp.dot(act, down[j], preferred_element_type=F32).astype(BF16)
            yield
        for z in range(4):
            looped(spread, z)
            yield

    def reduce(chunk):
        exchanges = {}
        for step in (2, 1, 3, 0):
            for p in range(3):
                one, two, three = ORDERS[p]
                index = window(coords, {one: WHOLE, two: WHOLE, three: (coords[three] + step) % 4}, ALL, REDUCE_PARTS[p])
                exchanges[p, step] = push(part.at[(chunk, 1 - core) + index], sib.at[(chunk,) + index],
                                          sib_send.at[chunk, p, step], sib_recv.at[chunk, p, step], sibling)

        def sweep(where, body):
            free = [axis for axis in range(3) if axis in where and where[axis] is WHOLE]

            def one(i):
                inner = (i // 4, i % 4) if len(free) == 2 else ((i,) if len(free) == 1 else ())
                spot = [where.get(axis, coords[axis]) for axis in range(3)]
                for axis, v in zip(free, inner):
                    spot[axis] = v
                body(tuple(spot), inner)

            if not free:
                one(0)
            else:
                def step(i, carry):
                    one(i)
                    return carry
                lax.fori_loop(0, 4 ** len(free), step, 0)

        class Ring:
            def __init__(self, p, number, axis, where, halves, fulls):
                self.p, self.base, self.axis, self.where = p, number * 6, axis, where
                self.halves, self.fulls = halves, fulls
                self.a = coords[axis]
                self.peers = (device(moved(coords, axis, 1), core), device(moved(coords, axis, 3), core))
                self.free = sum(v is WHOLE for v in where.values())
                self.came, self.tails = [], []

            def blocks(self, step):
                return {**self.where, self.axis: (self.a + step) % 4}

            def push(self, k, step, rows, which, side, lead):
                index = window(coords, self.blocks(step), rows, REDUCE_PARTS[self.p])
                dst = which.at[lead + (slice(None),) * self.free + (pl.ds(*rows), pl.ds(0, REDUCE_PARTS[self.p][1]))]
                n = self.base + k
                return push(part.at[(chunk, core) + index], dst,
                            rs_send.at[chunk, self.p, n], rs_recv.at[chunk, self.p, n], self.peers[side])

            def far(self):
                self.came = [self.push(0, 2, LO, self.halves, 0, ()), self.push(1, 2, HI, self.halves, 1, ())]

            def near(self, side):
                step, rows = ((1, HI), (3, LO))[side]
                self.tails.append(self.push(2 + side, step, rows, self.fulls, side, (side,)))

            def relay(self):
                cols = REDUCE_PARTS[self.p]
                for side, (step, rows) in enumerate(((1, LO), (3, HI))):
                    self.came[side].wait_recv()

                    def body(spot, inner, side=side, rows=rows):
                        spot = (chunk, core) + spot + (pl.ds(*rows), pl.ds(*cols))
                        part[spot] = part[spot] + self.halves[inner + (pl.ds(*rows), pl.ds(0, cols[1]))]
                    sweep(self.blocks(step), body)
                    self.tails.append(self.push(4 + side, step, rows, self.fulls, side, (side,)))

            def finish(self):
                cols = REDUCE_PARTS[self.p]
                for copy in self.tails:
                    copy.wait_recv()

                def body(spot, inner):
                    spot = (chunk, core) + spot + (slice(None), pl.ds(*cols))
                    one = self.fulls[(0,) + inner + (slice(None), pl.ds(0, cols[1]))].astype(F32)
                    two = self.fulls[(1,) + inner + (slice(None), pl.ds(0, cols[1]))].astype(F32)
                    part[spot] = (part[spot].astype(F32) + one + two).astype(BF16)
                sweep(self.blocks(0), body)

        outer, inner = [], []
        for p in range(3):
            one, two, three = ORDERS[p]
            outer.append(Ring(p, 0, three, {one: WHOLE, two: WHOLE}, near.at[chunk, p], far.at[chunk, p]))
            inner.append(Ring(p, 1, two, {one: WHOLE}, mnear.at[chunk, p], mfar.at[chunk, p]))

        def settle(p, step):
            cols = REDUCE_PARTS[p]
            exchanges[p, step].wait_recv()

            def body(spot, _):
                spot = spot + (slice(None), pl.ds(*cols))
                mine = (chunk, core) + spot
                part[mine] = part[mine] + sib[(chunk,) + spot]
            sweep(outer[p].blocks(step), body)

        yield
        for p in range(3):
            settle(p, 2)
            outer[p].far()
        yield
        for p in range(3):
            settle(p, 1)
            outer[p].near(0)
            settle(p, 3)
            outer[p].near(1)
        yield
        for p in range(3):
            outer[p].relay()
        yield
        for p in range(3):
            settle(p, 0)
        yield
        for p in range(3):
            outer[p].finish()
            inner[p].far()
            inner[p].near(0)
            inner[p].near(1)
        yield
        for p in range(3):
            inner[p].relay()
        yield
        ends = []
        for p in range(3):
            inner[p].finish()
            axis = ORDERS[p][0]
            copies = []
            for k in (1, 3, 2):
                index = window(coords, {axis: (coords[axis] + k) % 4}, ALL, REDUCE_PARTS[p])
                dst = first.at[chunk, p, k - 1, :, pl.ds(0, REDUCE_PARTS[p][1])]
                copies.append(push(part.at[(chunk, core) + index], dst, rs_send.at[chunk, p, 11 + k],
                                   rs_recv.at[chunk, p, 11 + k], device(moved(coords, axis, k), core)))
            ends.append(copies)
        yield
        for p in range(3):
            cols = REDUCE_PARTS[p]
            for copy in ends[p]:
                copy.wait_recv()
            total = part[(chunk, core) + coords + (slice(None), pl.ds(*cols))].astype(F32)
            for k in range(3):
                total = total + first[chunk, p, k, :, pl.ds(0, cols[1])].astype(F32)
            result[chunk, :, pl.ds(*cols)] = total.astype(BF16)

    def advance(process, count=1):
        for _ in range(count):
            next(process, None)

    gathers = [gather(0), gather(1)]
    return_own.wait_recv()
    advance(gathers[0])
    advance(gathers[1])
    advance(gathers[0])
    advance(gathers[0])
    advance(gathers[1])
    advance(gathers[0])
    advance(gathers[1])
    advance(gathers[0])
    advance(gathers[1])
    advance(gathers[0], 2)
    work = experts(0)
    advance(work, 8)
    advance(gathers[1])
    advance(work, 99)
    sums = [reduce(0), reduce(1)]
    advance(sums[0])
    advance(gathers[1])
    advance(sums[0], 2)
    advance(gathers[1])
    work = experts(1)
    advance(work, 2)
    advance(sums[0])
    advance(work, 2)
    advance(sums[0])
    advance(work, 1)
    advance(sums[0])
    advance(work, 1)
    advance(sums[0])
    advance(work, 2)
    advance(sums[0])
    advance(work, 99)
    advance(sums[1], 3)
    advance(sums[0], 99)
    advance(sums[1], 99)
    trade = push(result.at[1 - core], other, swap_send.at[1], swap_recv.at[1], sibling)
    trade.wait_recv()
    for h in range(2):
        cols = pl.ds(h * HALF, HALF)
        term = jnp.where(core == h, result[core].astype(F32), other[...].astype(F32))
        out[y, :, cols] = (mid[:, cols].astype(F32) + term).astype(BF16)
    final = [
        push(out.at[y], out.at[y], end_send.at[k - 1], end_recv.at[k - 1], device(moved(coords, 2, k), core))
        for k in (2, 1, 3)
    ]
    for copy in final:
        copy.wait_recv()
    for copy in pending:
        copy.wait_send()
    for b in range(4):
        out_ref[pl.ds(b * Q, Q), :] = out[b]


def moe(part, hidden, gain, aux, gate_up, down):
    wide = max(w for _, w in REDUCE_PARTS)
    dma = pltpu.SemaphoreType.DMA
    return pl.pallas_call(
        moe_kernel,
        name="moe",
        out_shape=(
            jax.ShapeDtypeStruct((ROWS, D), BF16),
            jax.ShapeDtypeStruct((2, 2, 4, 4, 4, Q, WIDE), BF16),
        ),
        in_specs=[pl.BlockSpec(memory_space=pltpu.VMEM)] * 4 + [pl.BlockSpec(memory_space=pltpu.HBM)] * 2,
        out_specs=(pl.BlockSpec(memory_space=pltpu.VMEM), pl.BlockSpec(memory_space=pltpu.HBM)),
        scratch_shapes=[
            pltpu.VMEM((3, Q, D), BF16),
            pltpu.VMEM((4, Q, WIDE), BF16),
            pltpu.VMEM((Q, D), BF16),
            pltpu.VMEM(gate_up.shape, BF16),
            pltpu.VMEM(down.shape, BF16),
            pltpu.VMEM((2, 2, 4, 4, Q, WIDE), BF16),
            pltpu.VMEM((2, SLOTS, D), BF16),
            pltpu.VMEM((2, SLOTS, D), BF16),
            pltpu.VMEM((8, 256, 128), BF16),
            pltpu.VMEM((2, SLOTS, 128), F32),
            pltpu.VMEM((2, 2, 4, 4, 4, Q, HALF), BF16),
            pltpu.VMEM((2, 4, 4, 4, Q, HALF), BF16),
            pltpu.VMEM((2, 3, 4, 4, Q, wide), BF16),
            pltpu.VMEM((2, 3, 2, 4, 4, Q, wide), BF16),
            pltpu.VMEM((2, 3, 4, Q, wide), BF16),
            pltpu.VMEM((2, 3, 2, 4, Q, wide), BF16),
            pltpu.VMEM((2, 3, 3, Q, wide), BF16),
            pltpu.VMEM((2, Q, HALF), BF16),
            pltpu.VMEM((Q, HALF), BF16),
            pltpu.VMEM((4, Q, D), BF16),
            dma((3,)),
            dma((3,)),
            dma((2, 3, 12)),
            dma((2, 3, 12)),
            dma((2, 3, 4)),
            dma((2, 3, 4)),
            dma((2,)),
            dma((2, 2)),
            dma((2,)),
            dma((2, 3, 4)),
            dma((2, 3, 4)),
            dma((2, 3, 15)),
            dma((2, 3, 15)),
            dma((2,)),
            dma((2,)),
            dma((3,)),
            dma((3,)),
        ],
        compiler_params=pltpu.CompilerParams(
            collective_id=0, has_side_effects=True, vmem_limit_bytes=VMEM_LIMIT
        ),
    )(part, hidden, gain, aux, gate_up, down)[0]


def rms_scale(inputs, gain):
    inputs = inputs.astype(F32)
    scaled = inputs * lax.rsqrt(jnp.mean(inputs * inputs, axis=-1, keepdims=True) + eps_norm)
    return (scaled * gain).astype(BF16)


def request_tables(new_lengths, prefix_lengths, row_count, cache_count):
    new_end = jnp.cumsum(new_lengths, dtype=jnp.int32)
    cache_end = jnp.cumsum(prefix_lengths, dtype=jnp.int32)
    token_index = jnp.arange(row_count, dtype=jnp.int32)
    cache_index = jnp.arange(cache_count, dtype=jnp.int32)
    token_request = jnp.sum(
        (token_index[:, None] >= new_end[None, :]).astype(jnp.int32), axis=1, dtype=jnp.int32
    )
    cache_request = jnp.sum(
        (cache_index[:, None] >= cache_end[None, :]).astype(jnp.int32), axis=1, dtype=jnp.int32
    )
    requests = new_lengths.shape[0]
    selector = token_request[:, None] == jnp.arange(requests, dtype=jnp.int32)[None, :]
    new_start = new_end - new_lengths
    offset = token_index - jnp.sum(
        jnp.where(selector, new_start[None, :], 0), axis=1, dtype=jnp.int32
    )
    position = offset + jnp.sum(
        jnp.where(selector, prefix_lengths[None, :], 0), axis=1, dtype=jnp.int32
    )
    return (token_request, cache_request, position)


def project_heads(normed, weight, gains, position, head_size):
    row_count = normed.shape[0]
    proj_width = weight.shape[2]
    full_width = proj_width * lax.axis_size("tp")
    by_member = jnp.transpose(weight, (1, 0, 2))
    projected = [
        jnp.dot(normed, by_member[m], preferred_element_type=F32) for m in range(3)
    ]
    squares = jnp.stack([jnp.sum(projected[m] * projected[m], axis=1) for m in range(2)], axis=1)
    totals = lax.psum(squares, "tp")
    inverse = lax.rsqrt(totals / full_width + eps_head)
    head_count = proj_width // head_size
    half_size = head_size // 2
    frequency = rope_base ** (-jnp.arange(half_size, dtype=F32) * 2.0 / head_size)
    angles = position.astype(F32)[:, None] * frequency[None, :]
    cosine = jnp.cos(angles)[:, None, :]
    sine_table = jnp.sin(angles)[:, None, :]
    outputs = []
    for member in range(2):
        member_rows = projected[member] * inverse[:, member : member + 1]
        portion = (member_rows * gains[member][None, :]).reshape(row_count, head_count, head_size)
        lower_half = portion[..., :half_size]
        upper_half = portion[..., half_size:]
        turned = jnp.concatenate(
            [
                lower_half * cosine - upper_half * sine_table,
                upper_half * cosine + lower_half * sine_table,
            ],
            axis=-1,
        )
        outputs.append(turned.reshape(row_count, proj_width).astype(BF16))
    outputs.append(projected[2].astype(BF16))
    return outputs


def attend(qkv, key_cache, value_cache, token_request, cache_request, head_size):
    row_count, proj_width = qkv[0].shape
    head_count = proj_width // head_size
    queries = qkv[0].reshape(row_count, head_count, head_size)
    key_rows = jnp.concatenate([key_cache, qkv[1]], axis=0).reshape(-1, head_count, head_size)
    value_rows = jnp.concatenate([value_cache, qkv[2]], axis=0).reshape(
        -1, head_count, head_size
    )
    scores = jnp.einsum(
        "qhd,khd->hqk", queries, key_rows, preferred_element_type=F32
    ) / math.sqrt(head_size)
    token_index = jnp.arange(row_count, dtype=jnp.int32)
    cache_ok = cache_request[None, :] == token_request[:, None]
    new_ok = (token_request[None, :] == token_request[:, None]) & (
        token_index[None, :] <= token_index[:, None]
    )
    allowed = jnp.concatenate([cache_ok, new_ok], axis=1)
    scores = jnp.where(allowed[None], scores, -1e30)
    row_max = jnp.max(scores, axis=-1, keepdims=True)
    weights = jnp.exp(scores - row_max)
    weights = (weights / jnp.sum(weights, axis=-1, keepdims=True)).astype(BF16)
    context = jnp.einsum("hqk,khd->qhd", weights, value_rows, preferred_element_type=F32)
    return context.reshape(row_count, proj_width).astype(BF16)


def weight_columns(expert_ids, expert_weights):
    experts = jnp.arange(NE, dtype=jnp.int32)[None, :]
    dense = jnp.zeros((expert_ids.shape[0], NE), F32)
    for k in range(expert_ids.shape[1]):
        dense = dense + jnp.where(expert_ids[:, k:k + 1] == experts, expert_weights[:, k:k + 1], 0.0)
    high = lax.reduce_precision(dense, 8, 7)
    return jnp.concatenate([high, dense - high], axis=1).astype(BF16)


def per_device(
    hidden_in,
    new_lengths,
    prefix_lengths,
    cache_keys,
    cache_values,
    attn_gain,
    w_qkv,
    norm_gains,
    w_out,
    moe_gain,
    expert_ids,
    expert_weights,
    w_gate_up,
    w_down,
    next_gain,
    next_qkv,
    next_norm_gains,
):
    row_count, model_width = hidden_in.shape
    cache_count = cache_keys.shape[0]
    token_request, cache_request, position = request_tables(
        new_lengths[0], prefix_lengths[0], row_count, cache_count
    )
    normed = rms_scale(hidden_in, attn_gain)
    qkv = project_heads(normed, w_qkv, norm_gains, position, HD)
    context = attend(qkv, cache_keys, cache_values, token_request, cache_request, HD)
    attn_part = jnp.dot(context, w_out, preferred_element_type=F32).astype(BF16)
    aux = weight_columns(expert_ids, expert_weights)
    hidden_out = moe(attn_part, hidden_in, moe_gain[None, :], aux, jnp.transpose(w_gate_up, (0, 2, 1, 3)), w_down)
    next_input = rms_scale(hidden_out, next_gain)
    next_out = project_heads(next_input, next_qkv, next_norm_gains, position, HD)
    return (hidden_out, jnp.stack(next_out, axis=1))


def solution(mesh):
    placed = (
        P("rep", None),
        P("rep", None),
        P("rep", None),
        P("rep", "tp"),
        P("rep", "tp"),
        P(),
        P(None, None, "tp"),
        P(None, "tp"),
        P("tp", None),
        P(),
        P("rep", None),
        P("rep", None),
        P("rep", None, None, "tp"),
        P("rep", "tp", None),
        P(),
        P(None, None, "tp"),
        P(None, "tp"),
    )
    return jax.shard_map(
        per_device,
        mesh=mesh,
        in_specs=placed,
        out_specs=(P("rep", None), P("rep", None, "tp")),
        check_vma=False,
    )
```

```python
import functools
import math

import jax
import jax.numpy as jnp
from jax import lax
from jax.experimental import pallas as pl
from jax.experimental.pallas import tpu as pltpu
from jax.sharding import PartitionSpec as P

HD = 128
MESH = pl.DeviceIdType.MESH
F32 = jnp.float32
BF16 = jnp.bfloat16

eps_norm = 1e-05
eps_head = 1e-06
rope_base = 10000.0

ROWS = 128
D = 2048
Q = 32
AUX = 128
HALF = D // 2
WIDE = HALF + AUX
NE = 64
CAP = 24
GATHER_PARTS = ((0, 384), (384, 384), (768, 384))
REDUCE_PARTS = ((0, 384), (384, 384), (768, 256))
ORDERS = ((1, 2, 0), (2, 0, 1), (0, 1, 2))
VMEM_LIMIT = 60 * 1024 * 1024


def place():
    rep = lax.axis_index("rep")
    return (rep // 8, (rep // 2) % 4, lax.axis_index("tp")), rep % 2


def device(coords, core):
    return (coords[0] * 8 + coords[1] * 2 + core, coords[2])


def moved(coords, axis, step):
    out = list(coords)
    out[axis] = (coords[axis] + step) % 4
    return tuple(out)


def greet(coords, core):
    barrier = pltpu.get_barrier_semaphore()
    peers = [device(coords, 1 - core)]
    for axis in range(3):
        for step in (1, 2, 3):
            peers.append(device(moved(coords, axis, step), core))
    for peer in peers:
        pl.semaphore_signal(barrier, inc=1, device_id=peer, device_id_type=MESH)
    pl.semaphore_wait(barrier, len(peers))


WHOLE = pl.ds(0, 4)
LO, HI, ALL = (0, 16), (16, 16), (0, Q)
WIDTH = 2 * CAP
SLOTS = 16 * CAP


def window(coords, at, rows, cols):
    index = tuple(at.get(axis, coords[axis]) for axis in range(3))
    return index + (pl.ds(*rows), pl.ds(*cols))


def moe_kernel(normed_ref, stream_ref, aux_ref, gu_hbm, down_hbm, out_ref, g_ref,
               own, gu, down, gbuf, xs, ys, hot, scale, part, sib,
               near, far, mnear, mfar, first, result, other, out,
               ag_send, ag_recv, share_send, share_recv, local_sem, load_sem, weight_sem,
               sib_send, sib_recv, rs_send, rs_recv, swap_send, swap_recv, end_send, end_recv):
    coords, core = place()
    rep = lax.axis_index("rep")
    y = coords[2]
    sibling = device(coords, 1 - core)
    pending = []
    fetch = [pltpu.make_async_copy(gu_hbm, gu, weight_sem.at[0]), pltpu.make_async_copy(down_hbm, down, weight_sem.at[1])]
    for copy in fetch:
        copy.start()
    greet(coords, core)

    def push(src, dst, send_sem, recv_sem, peer):
        copy = pltpu.make_async_remote_copy(
            src_ref=src, dst_ref=dst, send_sem=send_sem, recv_sem=recv_sem, device_id=peer, device_id_type=MESH)
        copy.start()
        pending.append(copy)
        return copy

    for h in range(2):
        own[2 + h, :, pl.ds(0, HALF)] = normed_ref[:, h * HALF:(h + 1) * HALF]
        own[2 + h, :, pl.ds(HALF, AUX)] = aux_ref[pl.ds(pl.multiple_of(y * Q, Q), Q), :]
    own[core] = own[2 + core]
    swap = push(own.at[2 + (1 - core)], own.at[core], swap_send.at[0], swap_recv.at[0], sibling)
    return_own = swap

    def gather(chunk):
        def at(index):
            return g_ref.at[(chunk, core) + index]

        arrivals = []

        def share(p, slot, index, src=None):
            arrivals.append(push(at(index) if src is None else src, at(index),
                                 share_send.at[chunk, p, slot], share_recv.at[chunk, p, slot], sibling))

        class Ring:
            def __init__(self, p, number, axis, where):
                self.p, self.base, self.axis, self.where = p, number * 4, axis, where
                self.a = coords[axis]
                self.right = device(moved(coords, axis, 1), core)
                self.left = device(moved(coords, axis, 3), core)
                self.ends = [self.push(0, self.index(0), self.right), self.push(1, self.index(0), self.left)]

            def index(self, step, rows=ALL):
                return window(coords, {**self.where, self.axis: (self.a + step) % 4}, rows, GATHER_PARTS[self.p])

            def push(self, k, index, peer):
                n = self.base + k
                return push(at(index), at(index), ag_send.at[chunk, self.p, n], ag_recv.at[chunk, self.p, n], peer)

            def near(self):
                for k, step, rows, peer in ((0, 3, LO, self.right), (1, 1, HI, self.left)):
                    self.ends[k].wait_recv()
                    self.ends.append(self.push(2 + k, self.index(step, rows), peer))

            def far(self):
                self.ends[2].wait_recv()
                self.ends[3].wait_recv()

        firsts = []
        for p in range(3):
            axis = ORDERS[p][0]
            index = window(coords, {}, ALL, GATHER_PARTS[p])
            src = own.at[chunk, :, pl.ds(*GATHER_PARTS[p])]
            firsts.append([
                push(src, at(index), ag_send.at[chunk, p, k - 1], ag_recv.at[chunk, p, k - 1],
                     device(moved(coords, axis, k), core))
                for k in (1, 3, 2)
            ])
        here = pltpu.make_async_copy(own.at[chunk], g_ref.at[(chunk, core) + coords], local_sem.at[chunk])
        here.start()
        yield
        here.wait()
        rings = []
        for p in range(3):
            for copy in firsts[p]:
                copy.wait_recv()
            rings.append(Ring(p, 1, ORDERS[p][1], {ORDERS[p][0]: WHOLE}))
        yield
        for ring in rings:
            ring.near()
        yield
        for p in range(3):
            one, two, three = ORDERS[p]
            rings[p].far()
            rings[p] = Ring(p, 2, three, {one: WHOLE, two: WHOLE})
            share(p, 0, rings[p].index(0))
        yield
        for p in range(3):
            rings[p].near()
            share(p, 1, rings[p].index(3))
            share(p, 2, rings[p].index(1))
        yield
        for p in range(3):
            rings[p].far()
            share(p, 3, rings[p].index(2))
        yield
        for copy in arrivals:
            copy.wait_recv()

    lane = lax.broadcasted_iota(jnp.int32, (256, 128), 1)
    second = (lax.broadcasted_iota(jnp.int32, (256, 1), 0) >= ROWS).astype(jnp.int32)
    slot_lane = lax.broadcasted_iota(jnp.int32, (WIDTH, 128), 1)

    def experts(chunk):
        def load(z):
            copies = [
                pltpu.make_async_copy(g_ref.at[chunk, h, z], gbuf.at[z % 2, h], load_sem.at[z % 2, h]) for h in range(2)
            ]
            for copy in copies:
                copy.start()
            return copies

        def collect(z, i):
            tri_r = lax.broadcasted_iota(jnp.int32, (256, 256), 0)
            tri_c = lax.broadcasted_iota(jnp.int32, (256, 256), 1)
            earlier = jnp.where((tri_c < tri_r) & ((tri_c >= ROWS) == (tri_r >= ROWS)), 1.0, 0.0).astype(BF16)
            blocks = pl.ds(2 * i, 2)
            low = gbuf[z % 2, 0, blocks].reshape(256, WIDE)
            high = gbuf[z % 2, 1, blocks].reshape(256, WIDE)[:, :HALF]
            chosen = jnp.where(low[:, HALF:].astype(F32) > 0, 1.0, 0.0)
            ranks = jnp.dot(earlier, chosen.astype(BF16), preferred_element_type=F32)
            match = jnp.zeros((256, 128), F32)
            for j in range(2):
                mine = lane == 2 * rep + j
                picked = jnp.sum(jnp.where(mine, chosen, 0.0), axis=1, keepdims=True)
                rank = jnp.sum(jnp.where(mine, ranks, 0.0), axis=1, keepdims=True).astype(jnp.int32)
                slot = jnp.where(picked > 0, rank + second * CAP + j * WIDTH, -1)
                match = match + jnp.where(lane == slot, 1.0, 0.0)
            hot[2 * z + i] = match.astype(BF16)
            select = match.T[:2 * WIDTH].astype(BF16)
            got_low = jnp.dot(select, low, preferred_element_type=F32)
            got_high = jnp.dot(select, high, preferred_element_type=F32)
            slots = pl.ds(pl.multiple_of((2 * z + i) * WIDTH, 16), WIDTH)
            for j in range(2):
                span = slice(j * WIDTH, (j + 1) * WIDTH)
                xs[j, slots, pl.ds(0, HALF)] = got_low[span, :HALF].astype(BF16)
                xs[j, slots, pl.ds(HALF, HALF)] = got_high[span].astype(BF16)
                mine = (slot_lane == 2 * rep + j) | (slot_lane == 2 * rep + j + NE)
                scale[j, slots, :] = jnp.broadcast_to(
                    jnp.sum(jnp.where(mine, got_low[span, HALF:], 0.0), axis=1, keepdims=True), (WIDTH, 128))

        def looped(body, z):
            def step(i, carry):
                body(z, i)
                return carry
            lax.fori_loop(0, 2, step, 0)

        def spread(z, i):
            slots = pl.ds(pl.multiple_of((2 * z + i) * WIDTH, 16), WIDTH)
            both = jnp.concatenate([ys[0, slots, :], ys[1, slots, :]], axis=0)
            back = jnp.dot(hot[2 * z + i][:, :2 * WIDTH], both, preferred_element_type=F32).astype(BF16)
            for h in range(2):
                part[chunk, h, z, pl.ds(2 * i, 2)] = back[:, h * HALF:(h + 1) * HALF].reshape(2, 4, Q, HALF)

        copies = load(0)
        for z in range(4):
            coming = load(z + 1) if z < 3 else None
            for copy in copies:
                copy.wait()
            looped(collect, z)
            copies = coming
            yield
        if chunk == 0:
            for copy in fetch:
                copy.wait()
        for j in range(2):
            x = xs[j]
            gate = jnp.dot(x, gu[j, 0], preferred_element_type=F32)
            up = jnp.dot(x, gu[j, 1], preferred_element_type=F32)
            act = gate / (1.0 + jnp.exp(-gate)) * up
            act = (act * scale[j][:, :1]).astype(BF16)
            ys[j] = jnp.dot(act, down[j], preferred_element_type=F32).astype(BF16)
            yield
        for z in range(4):
            looped(spread, z)
            yield

    def reduce(chunk):
        exchanges = {}
        for step in (2, 1, 3, 0):
            for p in range(3):
                one, two, three = ORDERS[p]
                index = window(coords, {one: WHOLE, two: WHOLE, three: (coords[three] + step) % 4}, ALL, REDUCE_PARTS[p])
                exchanges[p, step] = push(part.at[(chunk, 1 - core) + index], sib.at[(chunk,) + index],
                                          sib_send.at[chunk, p, step], sib_recv.at[chunk, p, step], sibling)

        def sweep(where, body):
            free = [axis for axis in range(3) if axis in where and where[axis] is WHOLE]

            def one(i):
                inner = (i // 4, i % 4) if len(free) == 2 else ((i,) if len(free) == 1 else ())
                spot = [where.get(axis, coords[axis]) for axis in range(3)]
                for axis, v in zip(free, inner):
                    spot[axis] = v
                body(tuple(spot), inner)

            if not free:
                one(0)
            else:
                def step(i, carry):
                    one(i)
                    return carry
                lax.fori_loop(0, 4 ** len(free), step, 0)

        class Ring:
            def __init__(self, p, number, axis, where, halves, fulls):
                self.p, self.base, self.axis, self.where = p, number * 6, axis, where
                self.halves, self.fulls = halves, fulls
                self.a = coords[axis]
                self.peers = (device(moved(coords, axis, 1), core), device(moved(coords, axis, 3), core))
                self.free = sum(v is WHOLE for v in where.values())
                self.came, self.tails = [], []

            def blocks(self, step):
                return {**self.where, self.axis: (self.a + step) % 4}

            def push(self, k, step, rows, which, side, lead):
                index = window(coords, self.blocks(step), rows, REDUCE_PARTS[self.p])
                dst = which.at[lead + (slice(None),) * self.free + (pl.ds(*rows), pl.ds(0, REDUCE_PARTS[self.p][1]))]
                n = self.base + k
                return push(part.at[(chunk, core) + index], dst,
                            rs_send.at[chunk, self.p, n], rs_recv.at[chunk, self.p, n], self.peers[side])

            def far(self):
                self.came = [self.push(0, 2, LO, self.halves, 0, ()), self.push(1, 2, HI, self.halves, 1, ())]

            def near(self, side):
                step, rows = ((1, HI), (3, LO))[side]
                self.tails.append(self.push(2 + side, step, rows, self.fulls, side, (side,)))

            def relay(self):
                cols = REDUCE_PARTS[self.p]
                for side, (step, rows) in enumerate(((1, LO), (3, HI))):
                    self.came[side].wait_recv()

                    def body(spot, inner, side=side, rows=rows):
                        spot = (chunk, core) + spot + (pl.ds(*rows), pl.ds(*cols))
                        part[spot] = part[spot] + self.halves[inner + (pl.ds(*rows), pl.ds(0, cols[1]))]
                    sweep(self.blocks(step), body)
                    self.tails.append(self.push(4 + side, step, rows, self.fulls, side, (side,)))

            def finish(self):
                cols = REDUCE_PARTS[self.p]
                for copy in self.tails:
                    copy.wait_recv()

                def body(spot, inner):
                    spot = (chunk, core) + spot + (slice(None), pl.ds(*cols))
                    one = self.fulls[(0,) + inner + (slice(None), pl.ds(0, cols[1]))].astype(F32)
                    two = self.fulls[(1,) + inner + (slice(None), pl.ds(0, cols[1]))].astype(F32)
                    part[spot] = (part[spot].astype(F32) + one + two).astype(BF16)
                sweep(self.blocks(0), body)

        outer, inner = [], []
        for p in range(3):
            one, two, three = ORDERS[p]
            outer.append(Ring(p, 0, three, {one: WHOLE, two: WHOLE}, near.at[chunk, p], far.at[chunk, p]))
            inner.append(Ring(p, 1, two, {one: WHOLE}, mnear.at[chunk, p], mfar.at[chunk, p]))

        def settle(p, step):
            cols = REDUCE_PARTS[p]
            exchanges[p, step].wait_recv()

            def body(spot, _):
                spot = spot + (slice(None), pl.ds(*cols))
                mine = (chunk, core) + spot
                part[mine] = part[mine] + sib[(chunk,) + spot]
            sweep(outer[p].blocks(step), body)

        yield
        for p in range(3):
            settle(p, 2)
            outer[p].far()
        yield
        for p in range(3):
            settle(p, 1)
            outer[p].near(0)
            settle(p, 3)
            outer[p].near(1)
        yield
        for p in range(3):
            outer[p].relay()
        yield
        for p in range(3):
            settle(p, 0)
        yield
        for p in range(3):
            outer[p].finish()
            inner[p].far()
            inner[p].near(0)
            inner[p].near(1)
        yield
        for p in range(3):
            inner[p].relay()
        yield
        ends = []
        for p in range(3):
            inner[p].finish()
            axis = ORDERS[p][0]
            copies = []
            for k in (1, 3, 2):
                index = window(coords, {axis: (coords[axis] + k) % 4}, ALL, REDUCE_PARTS[p])
                dst = first.at[chunk, p, k - 1, :, pl.ds(0, REDUCE_PARTS[p][1])]
                copies.append(push(part.at[(chunk, core) + index], dst, rs_send.at[chunk, p, 11 + k],
                                   rs_recv.at[chunk, p, 11 + k], device(moved(coords, axis, k), core)))
            ends.append(copies)
        yield
        for p in range(3):
            cols = REDUCE_PARTS[p]
            for copy in ends[p]:
                copy.wait_recv()
            total = part[(chunk, core) + coords + (slice(None), pl.ds(*cols))].astype(F32)
            for k in range(3):
                total = total + first[chunk, p, k, :, pl.ds(0, cols[1])].astype(F32)
            result[chunk, :, pl.ds(*cols)] = total.astype(BF16)

    def advance(process, count=1):
        for _ in range(count):
            next(process, None)

    gathers = [gather(0), gather(1)]
    return_own.wait_recv()
    advance(gathers[0])
    advance(gathers[1])
    advance(gathers[0])
    advance(gathers[0])
    advance(gathers[1])
    advance(gathers[0])
    advance(gathers[1])
    advance(gathers[0])
    advance(gathers[1])
    advance(gathers[0], 2)
    work = experts(0)
    advance(work, 8)
    advance(gathers[1])
    advance(work, 99)
    sums = [reduce(0), reduce(1)]
    advance(sums[0])
    advance(gathers[1])
    advance(sums[0], 2)
    advance(gathers[1])
    work = experts(1)
    advance(work, 2)
    advance(sums[0])
    advance(work, 2)
    advance(sums[0])
    advance(work, 1)
    advance(sums[0])
    advance(work, 1)
    advance(sums[0])
    advance(work, 2)
    advance(sums[0])
    advance(work, 99)
    advance(sums[1], 3)
    advance(sums[0], 99)
    advance(sums[1], 99)
    trade = push(result.at[1 - core], other, swap_send.at[1], swap_recv.at[1], sibling)
    trade.wait_recv()
    for h in range(2):
        cols = pl.ds(h * HALF, HALF)
        term = jnp.where(core == h, result[core].astype(F32), other[...].astype(F32))
        out[y, :, cols] = (stream_ref[:, cols].astype(F32) + term).astype(BF16)
    final = [
        push(out.at[y], out.at[y], end_send.at[k - 1], end_recv.at[k - 1], device(moved(coords, 2, k), core))
        for k in (2, 1, 3)
    ]
    for copy in final:
        copy.wait_recv()
    for copy in pending:
        copy.wait_send()
    for b in range(4):
        out_ref[pl.ds(b * Q, Q), :] = out[b]


def moe(normed, stream, aux, gate_up, down):
    wide = max(w for _, w in REDUCE_PARTS)
    dma = pltpu.SemaphoreType.DMA
    return pl.pallas_call(
        moe_kernel,
        name="moe",
        out_shape=(
            jax.ShapeDtypeStruct((ROWS, D), BF16),
            jax.ShapeDtypeStruct((2, 2, 4, 4, 4, Q, WIDE), BF16),
        ),
        in_specs=[pl.BlockSpec(memory_space=pltpu.VMEM)] * 3 + [pl.BlockSpec(memory_space=pltpu.HBM)] * 2,
        out_specs=(pl.BlockSpec(memory_space=pltpu.VMEM), pl.BlockSpec(memory_space=pltpu.HBM)),
        scratch_shapes=[
            pltpu.VMEM((4, Q, WIDE), BF16),
            pltpu.VMEM(gate_up.shape, BF16),
            pltpu.VMEM(down.shape, BF16),
            pltpu.VMEM((2, 2, 4, 4, Q, WIDE), BF16),
            pltpu.VMEM((2, SLOTS, D), BF16),
            pltpu.VMEM((2, SLOTS, D), BF16),
            pltpu.VMEM((8, 256, 128), BF16),
            pltpu.VMEM((2, SLOTS, 128), F32),
            pltpu.VMEM((2, 2, 4, 4, 4, Q, HALF), BF16),
            pltpu.VMEM((2, 4, 4, 4, Q, HALF), BF16),
            pltpu.VMEM((2, 3, 4, 4, Q, wide), BF16),
            pltpu.VMEM((2, 3, 2, 4, 4, Q, wide), BF16),
            pltpu.VMEM((2, 3, 4, Q, wide), BF16),
            pltpu.VMEM((2, 3, 2, 4, Q, wide), BF16),
            pltpu.VMEM((2, 3, 3, Q, wide), BF16),
            pltpu.VMEM((2, Q, HALF), BF16),
            pltpu.VMEM((Q, HALF), BF16),
            pltpu.VMEM((4, Q, D), BF16),
            dma((2, 3, 12)),
            dma((2, 3, 12)),
            dma((2, 3, 4)),
            dma((2, 3, 4)),
            dma((2,)),
            dma((2, 2)),
            dma((2,)),
            dma((2, 3, 4)),
            dma((2, 3, 4)),
            dma((2, 3, 15)),
            dma((2, 3, 15)),
            dma((2,)),
            dma((2,)),
            dma((3,)),
            dma((3,)),
        ],
        compiler_params=pltpu.CompilerParams(
            collective_id=1, has_side_effects=True, vmem_limit_bytes=VMEM_LIMIT
        ),
    )(normed, stream, aux, gate_up, down)[0]


def greet_row(coords, core):
    barrier = pltpu.get_barrier_semaphore()
    for k in (1, 2, 3):
        pl.semaphore_signal(barrier, inc=1, device_id=device(moved(coords, 2, k), core), device_id_type=MESH)
    pl.semaphore_wait(barrier, 3)


def send_to(src, dst, send_sem, recv_sem, peer):
    copy = pltpu.make_async_remote_copy(
        src_ref=src, dst_ref=dst, send_sem=send_sem, recv_sem=recv_sem, device_id=peer, device_id_type=MESH)
    copy.start()
    return copy


def trade_squares(projected, sums, inbox, send, recv, coords, core):
    lanes = lax.broadcasted_iota(jnp.int32, (ROWS, 128), 1)
    packed = jnp.zeros((ROWS, 128), F32)
    for m in range(2):
        packed = jnp.where(lanes == m, jnp.sum(projected[m] * projected[m], axis=1, keepdims=True), packed)
    sums[...] = packed.T[:8]
    return [
        send_to(sums, inbox.at[k - 1], send.at[k - 1], recv.at[k - 1], device(moved(coords, 2, k), core))
        for k in (2, 1, 3)
    ]


def total_squares(copies, sums, inbox):
    for copy in copies:
        copy.wait_recv()
    total = sums[...] + inbox[0] + inbox[1] + inbox[2]
    inverse = lax.rsqrt(total / D + eps_head)
    return jnp.concatenate([inverse, jnp.zeros((120, 128), F32)], axis=0).T


def turn(rows, inverse, gains, cosine, sine):
    heads = []
    scaled = rows * inverse * gains
    for h in range(rows.shape[1] // HD):
        v = scaled[:, h * HD:(h + 1) * HD]
        heads.append((v * cosine + pltpu.roll(v, HD // 2, 1) * sine).astype(BF16))
    return heads


def norm_rows(rows, gain):
    wide = rows.astype(F32)
    return (wide * lax.rsqrt(jnp.mean(wide * wide, axis=-1, keepdims=True) + eps_norm) * gain).astype(BF16)


def attention_kernel(new_ref, prefix_ref, hidden_ref, gain_ref, w_hbm, head_gain_ref, keys_hbm, values_hbm, wo_hbm,
                     moe_gain_ref, freq_ref, normed_ref, stream_ref, cos_ref, sin_ref,
                     w, keys, values, wo, sums, inbox, part, half, full,
                     w_sem, cache_sem, sum_send, sum_recv, send, recv):
    coords, core = place()
    y = coords[2]
    fetch = [pltpu.make_async_copy(w_hbm.at[m], w.at[m], w_sem.at[m]) for m in range(3)]
    fetch += [
        pltpu.make_async_copy(keys_hbm, keys, cache_sem.at[0]),
        pltpu.make_async_copy(values_hbm, values, cache_sem.at[1]),
        pltpu.make_async_copy(wo_hbm, wo, cache_sem.at[2]),
    ]
    for copy in fetch:
        copy.start()
    greet_row(coords, core)
    normed = norm_rows(hidden_ref[...], gain_ref[...])
    projected = []
    for m in range(2):
        fetch[m].wait()
        projected.append(jnp.dot(normed, w[m], preferred_element_type=F32))
    copies = trade_squares(projected, sums, inbox, sum_send, sum_recv, coords, core)
    fetch[2].wait()
    fresh = jnp.dot(normed, w[2], preferred_element_type=F32).astype(BF16)

    token = lax.broadcasted_iota(jnp.int32, (ROWS, 1), 0)
    token_row = lax.broadcasted_iota(jnp.int32, (1, ROWS), 1)
    cached = lax.broadcasted_iota(jnp.int32, (1, keys.shape[0]), 1)
    position = token
    request, request_row, cache_request = jnp.zeros_like(token), jnp.zeros_like(token_row), jnp.zeros_like(cached)
    end, cache_end = 0, 0
    for s in range(new_ref.shape[1]):
        begin = end
        end = end + new_ref[0, s]
        cache_end = cache_end + prefix_ref[0, s]
        inside = (token >= begin) & (token < end)
        position = position + jnp.where(inside, prefix_ref[0, s] - begin, 0)
        request = request + (token >= end).astype(jnp.int32)
        request_row = request_row + (token_row >= end).astype(jnp.int32)
        cache_request = cache_request + (cached >= cache_end).astype(jnp.int32)
    angles = position.astype(F32) * freq_ref[...]
    side = lax.broadcasted_iota(jnp.int32, (ROWS, HD), 1)
    cosine = jnp.cos(angles)
    sine = jnp.where(side < HD // 2, -1.0, 1.0) * jnp.sin(angles)
    cos_ref[...] = cosine
    sin_ref[...] = sine
    cache_ok = cache_request == request
    new_ok = (request_row == request) & (token_row <= token)
    inverse = total_squares(copies, sums, inbox)
    gains = head_gain_ref[...]
    query_heads = turn(projected[0], inverse[:, 0:1], gains[0:1], cosine, sine)
    key_heads = turn(projected[1], inverse[:, 1:2], gains[1:2], cosine, sine)
    for n in (3, 4):
        fetch[n].wait()
    contract = (((1,), (1,)), ((), ()))
    context = []
    for h in range(len(query_heads)):
        cols = pl.ds(h * HD, HD)
        old = lax.dot_general(query_heads[h], keys[:, cols], contract, preferred_element_type=F32)
        new = lax.dot_general(query_heads[h], key_heads[h], contract, preferred_element_type=F32)
        old = jnp.where(cache_ok, old * (1.0 / math.sqrt(HD)), -1e30)
        new = jnp.where(new_ok, new * (1.0 / math.sqrt(HD)), -1e30)
        top = jnp.maximum(jnp.max(old, axis=1, keepdims=True), jnp.max(new, axis=1, keepdims=True))
        old = jnp.exp(old - top)
        new = jnp.exp(new - top)
        total = jnp.sum(old, axis=1, keepdims=True) + jnp.sum(new, axis=1, keepdims=True)
        scale = 1.0 / total
        mixed = jnp.dot((old * scale).astype(BF16), values[:, cols], preferred_element_type=F32)
        mixed = mixed + jnp.dot(
            (new * scale).astype(BF16), fresh[:, h * HD:(h + 1) * HD], preferred_element_type=F32)
        context.append(mixed.astype(BF16))
    fetch[5].wait()
    out = jnp.dot(jnp.concatenate(context, axis=1), wo[...], preferred_element_type=F32).astype(BF16)
    for b in range(4):
        part[b] = out[b * Q:(b + 1) * Q]
    right, left = device(moved(coords, 2, 1), core), device(moved(coords, 2, 3), core)
    low, high = pl.ds(0, 16), pl.ds(16, 16)
    across, after, before = (y + 2) % 4, (y + 1) % 4, (y + 3) % 4
    sends = [
        send_to(part.at[across, low], half.at[low], send.at[0], recv.at[0], right),
        send_to(part.at[across, high], half.at[high], send.at[1], recv.at[1], left),
        send_to(part.at[after, high], full.at[0, high], send.at[2], recv.at[2], right),
        send_to(part.at[before, low], full.at[1, low], send.at[3], recv.at[3], left),
    ]
    sends[0].wait_recv()
    part[after, low] = part[after, low] + half[low]
    sends.append(send_to(part.at[after, low], full.at[0, low], send.at[4], recv.at[4], right))
    sends[1].wait_recv()
    part[before, high] = part[before, high] + half[high]
    sends.append(send_to(part.at[before, high], full.at[1, high], send.at[5], recv.at[5], left))
    for copy in sends[2:]:
        copy.wait_recv()
    rows = pl.ds(pl.multiple_of(y * Q, Q), Q)
    stream = hidden_ref[rows, :].astype(F32) + (
        part[y].astype(F32) + full[0].astype(F32) + full[1].astype(F32))
    stream = stream.astype(BF16)
    stream_ref[...] = stream
    normed_ref[...] = norm_rows(stream, moe_gain_ref[...])
    for copy in copies + sends:
        copy.wait_send()


def frequencies():
    half = HD // 2
    frequency = rope_base ** (-jnp.arange(half, dtype=F32) * 2.0 / HD)
    return jnp.concatenate([frequency, frequency])[None, :]


def attention(new_lengths, prefix_lengths, hidden, gain, weight, head_gains, keys, values, w_out, moe_gain):
    dma = pltpu.SemaphoreType.DMA
    vmem, smem, hbm = (pl.BlockSpec(memory_space=s) for s in (pltpu.VMEM, pltpu.SMEM, pltpu.HBM))
    return pl.pallas_call(
        attention_kernel,
        name="attention",
        out_shape=(
            jax.ShapeDtypeStruct((Q, D), BF16),
            jax.ShapeDtypeStruct((Q, D), BF16),
            jax.ShapeDtypeStruct((ROWS, HD), F32),
            jax.ShapeDtypeStruct((ROWS, HD), F32),
        ),
        in_specs=[smem, smem, vmem, vmem, hbm, vmem, hbm, hbm, hbm, vmem, vmem],
        out_specs=(vmem,) * 4,
        scratch_shapes=[
            pltpu.VMEM(weight.shape, BF16),
            pltpu.VMEM(keys.shape, BF16),
            pltpu.VMEM(values.shape, BF16),
            pltpu.VMEM(w_out.shape, BF16),
            pltpu.VMEM((8, 128), F32),
            pltpu.VMEM((3, 8, 128), F32),
            pltpu.VMEM((4, Q, D), BF16),
            pltpu.VMEM((Q, D), BF16),
            pltpu.VMEM((2, Q, D), BF16),
            dma((3,)),
            dma((3,)),
            dma((3,)),
            dma((3,)),
            dma((6,)),
            dma((6,)),
        ],
        compiler_params=pltpu.CompilerParams(
            collective_id=0, has_side_effects=True, vmem_limit_bytes=VMEM_LIMIT
        ),
    )(new_lengths, prefix_lengths, hidden, gain, weight, head_gains, keys, values, w_out, moe_gain, frequencies())


def next_kernel(hidden_ref, gain_ref, w_hbm, head_gain_ref, cos_ref, sin_ref, out_ref,
                w, sums, inbox, w_sem, sum_send, sum_recv):
    coords, core = place()
    fetch = [pltpu.make_async_copy(w_hbm.at[m], w.at[m], w_sem.at[m]) for m in range(3)]
    for copy in fetch:
        copy.start()
    greet_row(coords, core)
    normed = norm_rows(hidden_ref[...], gain_ref[...])
    projected = []
    for m in range(2):
        fetch[m].wait()
        projected.append(jnp.dot(normed, w[m], preferred_element_type=F32))
    copies = trade_squares(projected, sums, inbox, sum_send, sum_recv, coords, core)
    fetch[2].wait()
    out_ref[2] = jnp.dot(normed, w[2], preferred_element_type=F32).astype(BF16)
    inverse = total_squares(copies, sums, inbox)
    gains = head_gain_ref[...]
    for m in range(2):
        heads = turn(projected[m], inverse[:, m:m + 1], gains[m:m + 1], cos_ref[...], sin_ref[...])
        for h, rows in enumerate(heads):
            out_ref[m, :, pl.ds(h * HD, HD)] = rows
    for copy in copies:
        copy.wait_send()


def next_heads(hidden, gain, weight, head_gains, cosine, sine):
    dma = pltpu.SemaphoreType.DMA
    vmem, hbm = (pl.BlockSpec(memory_space=s) for s in (pltpu.VMEM, pltpu.HBM))
    return pl.pallas_call(
        next_kernel,
        name="next_heads",
        out_shape=jax.ShapeDtypeStruct((3, ROWS, weight.shape[2]), BF16),
        in_specs=[vmem, vmem, hbm, vmem, vmem, vmem],
        out_specs=vmem,
        scratch_shapes=[
            pltpu.VMEM(weight.shape, BF16),
            pltpu.VMEM((8, 128), F32),
            pltpu.VMEM((3, 8, 128), F32),
            dma((3,)),
            dma((3,)),
            dma((3,)),
        ],
        compiler_params=pltpu.CompilerParams(
            collective_id=2, has_side_effects=True, vmem_limit_bytes=VMEM_LIMIT
        ),
    )(hidden, gain, weight, head_gains, cosine, sine)


def weight_columns(expert_ids, expert_weights):
    experts = jnp.arange(NE, dtype=jnp.int32)[None, :]
    dense = jnp.zeros((expert_ids.shape[0], NE), F32)
    for k in range(expert_ids.shape[1]):
        dense = dense + jnp.where(expert_ids[:, k:k + 1] == experts, expert_weights[:, k:k + 1], 0.0)
    high = lax.reduce_precision(dense, 8, 7)
    return jnp.concatenate([high, dense - high], axis=1).astype(BF16)


def per_device(
    hidden_in,
    new_lengths,
    prefix_lengths,
    cache_keys,
    cache_values,
    attn_gain,
    w_qkv,
    norm_gains,
    w_out,
    moe_gain,
    expert_ids,
    expert_weights,
    w_gate_up,
    w_down,
    next_gain,
    next_qkv,
    next_norm_gains,
):
    by_member = (1, 0, 2)
    normed, stream, cosine, sine = attention(
        new_lengths, prefix_lengths, hidden_in, attn_gain[None, :], jnp.transpose(w_qkv, by_member), norm_gains,
        cache_keys, cache_values, w_out, moe_gain[None, :])
    aux = weight_columns(expert_ids, expert_weights)
    hidden_out = moe(normed, stream, aux, jnp.transpose(w_gate_up, (0, 2, 1, 3)), w_down)
    next_out = next_heads(
        hidden_out, next_gain[None, :], jnp.transpose(next_qkv, by_member), next_norm_gains, cosine, sine)
    return (hidden_out, jnp.transpose(next_out, by_member))


def solution(mesh):
    placed = (
        P("rep", None),
        P("rep", None),
        P("rep", None),
        P("rep", "tp"),
        P("rep", "tp"),
        P(),
        P(None, None, "tp"),
        P(None, "tp"),
        P("tp", None),
        P(),
        P("rep", None),
        P("rep", None),
        P("rep", None, None, "tp"),
        P("rep", "tp", None),
        P(),
        P(None, None, "tp"),
        P(None, "tp"),
    )
    return jax.shard_map(
        per_device,
        mesh=mesh,
        in_specs=placed,
        out_specs=(P("rep", None), P("rep", None, "tp")),
        check_vma=False,
    )
```
